32 devices in a mesh: groups: 2 (over y), pos: 4 (over z), strand: 2 (over core), heads: 2 (over x).
Axes of the slice: x: 2, y: 2, z: 4, core: 2. Of those that a mesh axis runs over, the one named last changes fastest.
Arguments:
- base_codes: int32 [131072], P(('groups', 'pos')), parts along dimension 0, may hold values from 0 to 3
- embed_table: bfloat16 [512, 1536], P(None, 'heads'), may hold values from -0.5 to 0.5
- attn_gain: float32 [1536], replicated, may hold values from 0.1 to 1.9
- w_query: bfloat16 [1536, 1024], P(None, 'heads')
- w_key: bfloat16 [1536, 128], P(None, 'heads')
- w_value: bfloat16 [1536, 192], P(None, 'heads'), may hold values from -0.15625 to 0.15625
- w_out: bfloat16 [1536, 1536], P('heads'), may hold values from -0.15625 to 0.15625
- head_gain: float32 [1536], replicated, may hold values from 0.1 to 1.9
- w_tracks: bfloat16 [1536, 2, 1536], P(None, None, 'heads'), may hold values from -0.15625 to 0.15625
- track_pairs: int32 [3072], P(('strand', 'heads')), may hold values from 0 to 3071, as said below
Outputs:
- tracks_out: float32 [1024, 3072], P(('groups', 'pos'), ('strand', 'heads')), parts along dimension 0
The draws below stay inside these ranges and needn't reach their ends.
There are 2 independent parts, one for each index of `groups`. The reference program is written for one: setup_inputs(seed, part) draws one part's arguments, and reference() takes and returns one part's arrays. A program takes and returns all parts, laid end to end along the dimension named above; an argument that names none is the same for every part. Nothing has to cross between parts.
Inputs may be any that keep to these rules, and one draw needn't show every extreme that they name: track_pairs is an involution: each aligned pair of tracks 2 j and 2 j + 1 is either swapped or left in place.
All inputs are finite; a program needn't handle non-finite values.
Results may differ from the reference program's by a relative error of at most 0.008.
Values may be sent and summed in bfloat16 or wider, within the bound.
A program may use at most 64 MiB of HBM per device.

```python
import math
import jax
import jax.numpy as jnp
from jax import lax

D = 1536
HEADS = 8
KDIM = 128
VDIM = 192
TRACKS = 3072
BIN = 128
LEN = 512


def key_matrix(key):
    return jax.random.normal(jax.random.fold_in(key, 11), (D, KDIM), jnp.float32) * D ** (-0.5)


def draw_w_key(key, part):
    return key_matrix(key).astype(jnp.bfloat16)


def draw_w_query(key, part):
    base_draw = jax.random.normal(jax.random.fold_in(key, 23), (D, HEADS, KDIM), jnp.float32) * D ** (-0.5)
    spread = jax.random.uniform(jax.random.fold_in(key, 29), (HEADS,), jnp.float32, 1.0, 3.0)
    base_draw = base_draw * spread[None, :, None]
    return base_draw.reshape(D, HEADS * KDIM).astype(jnp.bfloat16)


def draw_track_pairs(key, part):
    flips = jax.random.randint(jax.random.fold_in(key, 41), (TRACKS // 2,), 0, 2, dtype=jnp.int32)
    indices = jnp.arange(TRACKS, dtype=jnp.int32)
    return indices + jnp.repeat(flips, 2) * (1 - 2 * (indices % 2))


def touch_ends(entries, rng, least, top_value):
    place = [jax.random.randint(jax.random.fold_in(rng, axis), (), 0, length) for axis, length in enumerate(entries.shape)]
    widest = entries.shape.index(max(entries.shape))
    beside = place[:widest] + [(place[widest] + 1) % entries.shape[widest]] + place[widest + 1:]
    return entries.at[tuple(place)].set(least).at[tuple(beside)].set(top_value)


def shard_levels(rng, dims, pieces, smallest, largest):
    loudness, own = 1.0, jax.random.fold_in(rng, 6)
    for position, blocks in pieces:
        heights = jnp.exp(jax.random.uniform(jax.random.fold_in(own, position), (blocks,), jnp.float32, smallest / len(pieces), largest / len(pieces)))
        loudness = loudness * jnp.repeat(heights, dims[position] // blocks).reshape([-1 if axis == position else 1 for axis in range(len(dims))])
    return loudness


def centred(rng, shape, width, reach, pieces=(), kind=jnp.bfloat16):
    drawn = jax.random.normal(rng, shape, jnp.float32) * width
    if len(pieces) > 0:
        drawn = shard_levels(rng, shape, pieces, -0.22, 0.18) * drawn
    return jnp.clip(drawn, min=-reach, max=reach).astype(kind)


def setup_inputs(seed: int = 0, part: int = 0) -> dict:
    keys = jax.random.split(jax.random.key(seed), 11)
    part_keys = jax.random.split(jax.random.fold_in(keys[10], part), 11)
    base_codes = touch_ends(jax.random.randint(part_keys[0], (LEN * BIN,), 0, 4), jax.random.fold_in(part_keys[0], 1), 0, 3).astype(jnp.int32)
    embed_table = centred(keys[1], (BIN * 4, D), BIN ** -0.5, 0.5, ((1, 2),))
    attn_gain = jnp.clip(1.0 + 0.18 * jax.random.normal(keys[2], (D,), jnp.float32), 0.1, 1.9)
    w_query = draw_w_query(jax.random.fold_in(keys[10], 71), part)
    w_key = draw_w_key(jax.random.fold_in(keys[10], 71), part)
    w_value = centred(keys[5], (D, VDIM), D ** -0.5, 0.15625, ((1, 2),))
    w_out = centred(keys[6], (HEADS * VDIM, D), (HEADS * VDIM) ** -0.5, 0.15625, ((0, 2),))
    head_gain = jnp.clip(1.0 + 0.18 * jax.random.normal(keys[7], (D,), jnp.float32), 0.1, 1.9)
    w_tracks = centred(keys[8], (D, 2, TRACKS // 2), D ** -0.5, 0.15625, ((2, 2),))
    track_pairs = draw_track_pairs(jax.random.fold_in(keys[10], 71), part)
    return {"base_codes": base_codes, "embed_table": embed_table, "attn_gain": attn_gain, "w_query": w_query, "w_key": w_key, "w_value": w_value, "w_out": w_out, "head_gain": head_gain, "w_tracks": w_tracks, "track_pairs": track_pairs}


def rotate(values, positions):
    row_total = values.shape[0]
    head_total = values.shape[1] // KDIM
    half_dim = KDIM // 2
    inverse = jnp.exp(jnp.arange(half_dim, dtype=jnp.float32) * (-math.log(10000.0) / half_dim))
    angles = positions.astype(jnp.float32)[:, None] * inverse[None, :]
    cosine = jnp.cos(angles)[:, None, :]
    sine_val = jnp.sin(angles)[:, None, :]
    shaped = values.astype(jnp.float32).reshape(row_total, head_total, KDIM)
    low_part = shaped[:, :, :half_dim]
    high_part = shaped[:, :, half_dim:]
    turned = jnp.concatenate([low_part * cosine - high_part * sine_val, high_part * cosine + low_part * sine_val], axis=2)
    return turned.reshape(row_total, head_total * KDIM).astype(jnp.bfloat16)

def embed_bases(base_block, lookup):
    onehot = (base_block[:, :, None] == jnp.arange(4, dtype=jnp.int32)[None, None, :]).astype(jnp.bfloat16)
    onehot = onehot.reshape(base_block.shape[0], base_block.shape[1] * 4)
    return jnp.dot(onehot, lookup, preferred_element_type=jnp.float32).astype(jnp.bfloat16)

def normalize(values, gain_vec):
    floats = values.astype(jnp.float32)
    square = lax.optimization_barrier(jnp.mean(floats * floats, axis=-1, keepdims=True))
    return (floats * lax.rsqrt(square + 1e-06) * gain_vec).astype(jnp.bfloat16)

def strand_pass(inputs, positions, attn_gain, w_query, w_key, w_value, w_out, head_gain, w_tracks):
    normed = normalize(inputs, attn_gain)
    queries = rotate(jnp.dot(normed, w_query, preferred_element_type=jnp.float32).astype(jnp.bfloat16), positions)
    keys_rot = rotate(jnp.dot(normed, w_key, preferred_element_type=jnp.float32).astype(jnp.bfloat16), positions)
    values = jnp.dot(normed, w_value, preferred_element_type=jnp.float32).astype(jnp.bfloat16)
    per_head = queries.reshape(LEN, HEADS, KDIM).transpose(1, 0, 2)

    def attend(query_block):
        scores = jnp.dot(query_block, keys_rot.T, preferred_element_type=jnp.float32) * KDIM ** (-0.5)
        top_score = lax.optimization_barrier(jnp.max(scores, axis=1, keepdims=True))
        weights = jnp.exp(scores - top_score)
        weight_sum = lax.optimization_barrier(jnp.sum(weights, axis=1, keepdims=True))
        weighted = jnp.dot(weights.astype(jnp.bfloat16), values, preferred_element_type=jnp.float32)
        return (weighted / weight_sum).astype(jnp.bfloat16)
    outputs = lax.map(attend, per_head)
    merged = outputs.transpose(1, 0, 2).reshape(LEN, HEADS * VDIM)
    mixed_sum = jnp.dot(merged, w_out, preferred_element_type=jnp.float32)
    hidden = (inputs.astype(jnp.float32) + mixed_sum).astype(jnp.bfloat16)
    normed_out = normalize(hidden, head_gain)
    logits = jnp.dot(normed_out, w_tracks.reshape(D, TRACKS), preferred_element_type=jnp.float32)
    return jax.nn.softplus(logits).astype(jnp.bfloat16)

def reference(base_codes, embed_table, attn_gain, w_query, w_key, w_value, w_out, head_gain, w_tracks, track_pairs):
    base_block = base_codes.reshape(LEN, BIN)
    flipped = 3 - base_block[::-1, ::-1]
    positions = jnp.arange(LEN, dtype=jnp.int32)
    forward = strand_pass(embed_bases(base_block, embed_table), positions, attn_gain, w_query, w_key, w_value, w_out, head_gain, w_tracks)
    reverse = strand_pass(embed_bases(flipped, embed_table), positions, attn_gain, w_query, w_key, w_value, w_out, head_gain, w_tracks)
    aligned = jnp.take(reverse[::-1], track_pairs, axis=1)
    return 0.5 * (forward.astype(jnp.float32) + aligned.astype(jnp.float32))
```

```python
import functools
import math

import jax
import jax.numpy as jnp
from jax import lax
from jax.experimental import pallas as pl
from jax.experimental.pallas import tpu as pltpu
from jax.sharding import PartitionSpec as P

KDIM = 128
VDIM = 192
BIN = 128
F32 = jnp.float32
BF16 = jnp.bfloat16
MESH = pl.DeviceIdType.MESH
NT = (((1,), (1,)), ((), ()))
FIRST = 1


def spread(table, first, count):
    return jnp.concatenate([table[first + i : first + i + 1, :] for i in range(count)], axis=1)


def partner(z, step, N):
    if N & (N - 1):
        return lax.rem(z + step, N)
    bit = 1
    while bit < N:
        if step & bit:
            z = z + bit - 2 * bit * ((z // bit) % 2)
        bit *= 2
    return z


def farthest(z, k, N):
    up = (N - 1 - z - k + N - 1) // N
    return up * (N - 1 - k) + (1 - up) * (k + z - (N - 1))


def kernel(
    H, N, NC, NX,
    codes_hbm, et_hbm, g1_hbm, wq_hbm, wk_hbm, wv_hbm, wo_hbm, g2_hbm, wt_hbm, tp_hbm,
    out_ref, tp_out,
    codes_ref, g1_ref, g2_ref, et, wq, wkv, wo, wraw, wt, xbuf, kvbuf, tabc, tabs, own, psend, precv, lg, snd, rcv,
    wsem, xs, xr, kvs, kvr, kfs, kds, ps, pr, ss, sr, ready, turn,
):
    h = lax.axis_index("heads")
    z = lax.axis_index("pos")
    strand = lax.axis_index("strand")
    rows = codes_hbm.shape[0]
    dl = et.shape[1]
    D = dl * H
    kl = wk_hbm.shape[0]
    kvl = wkv.shape[0]
    lh = wq.shape[1] // KDIM
    cols = wt.shape[2]
    total = rows * N

    hp = [lax.rem(h + i, H) for i in range(1, H)]
    zp = [partner(z, i, N) for i in range(1, N)]
    other_strand = 1 - strand

    def direct(p):
        return (strand != FIRST) | (abs(p - z) == N - 1)

    barrier = pltpu.get_barrier_semaphore()

    def greet(sem, up):
        for peer in zp:
            @pl.when(peer > z if up else peer < z)
            def _():
                for other in [h] + hp:
                    pl.semaphore_signal(
                        sem, inc=1, device_id={"pos": peer, "heads": other}, device_id_type=MESH
                    )

    greet(barrier, True)
    for peer in hp:
        pl.semaphore_signal(barrier, inc=1, device_id={"heads": peer}, device_id_type=MESH)
    pl.semaphore_signal(barrier, inc=1, device_id={"strand": other_strand}, device_id_type=MESH)

    loads = [
        pltpu.make_async_copy(et_hbm, et, wsem.at[0]),
        pltpu.make_async_copy(wk_hbm, wkv.at[pl.ds(0, kl), :], wsem.at[1]),
        pltpu.make_async_copy(wv_hbm, wkv.at[pl.ds(kl, kvl - kl), :], wsem.at[2]),
        pltpu.make_async_copy(wq_hbm, wq, wsem.at[3]),
        pltpu.make_async_copy(wo_hbm, wo, wsem.at[4]),
        pltpu.make_async_copy(wt_hbm, wraw, wsem.at[5]),
        pltpu.make_async_copy(codes_hbm, codes_ref, wsem.at[6]),
        pltpu.make_async_copy(g1_hbm, g1_ref, wsem.at[7]),
        pltpu.make_async_copy(g2_hbm, g2_ref, wsem.at[8]),
        pltpu.make_async_copy(tp_hbm, tp_out, wsem.at[9]),
    ]
    loads[6].start()
    loads[0].start()
    loads[7].start()
    loads[8].start()
    loads[9].start()

    fwd = strand == 0
    width = 4 * BIN
    src_row = lax.broadcasted_iota(jnp.int32, (BIN, width), 0)
    place = lax.broadcasted_iota(jnp.int32, (BIN, width), 1) // 4
    want = jnp.where(fwd, place, BIN - 1 - place)
    expand = (src_row == want).astype(F32).astype(BF16)
    loads[6].wait()
    repeated = jnp.dot(codes_ref[...].astype(F32).astype(BF16), expand, preferred_element_type=F32)
    letter = lax.broadcasted_iota(jnp.int32, (rows, width), 1) % 4
    letter = jnp.where(fwd, letter, 3 - letter).astype(F32)
    onehot = (repeated == letter).astype(F32).astype(BF16)

    loads[0].wait()
    for k in (1, 2, 3, 5, 4):
        loads[k].start()
    xw = dl // NX
    sends = []

    def x_copy(i, c):
        return pltpu.make_async_remote_copy(
            xbuf.at[h, c], xbuf.at[h, c], xs.at[i, c], xr.at[h, c],
            device_id={"heads": hp[i]}, device_id_type=MESH,
        )

    for c in range(NX):
        part = jnp.dot(onehot, et[:, c * xw : (c + 1) * xw], preferred_element_type=F32)
        xbuf[h, c] = part.astype(BF16)
        if c == 0:
            pl.semaphore_wait(barrier, len(hp) + 1 + z * H)
            greet(ready, False)

        @pl.when(strand == FIRST)
        def _():
            for i in range(len(hp)):
                x_copy(i, c).start()

    half = KDIM // 2
    step = -math.log(10000.0) / half
    lane_pos = lax.broadcasted_iota(jnp.int32, (half, rows), 1)
    kinv = jnp.exp(lax.broadcasted_iota(jnp.int32, (half, rows), 0).astype(F32) * step)
    for p in range(N):
        pos = lane_pos + p * rows
        pos = jnp.where(fwd, pos, total - 1 - pos).astype(F32)
        tabc[p] = jnp.cos(pos * kinv)
        tabs[p] = jnp.sin(pos * kinv)
    qpos = lax.broadcasted_iota(jnp.int32, (rows, KDIM), 0) + z * rows
    qpos = jnp.where(fwd, qpos, total - 1 - qpos).astype(F32)
    qlane = lax.broadcasted_iota(jnp.int32, (rows, KDIM), 1)
    qang = qpos * jnp.exp((qlane % half).astype(F32) * step)
    qcos = jnp.cos(qang)
    qsin = jnp.where(qlane < half, -1.0, 1.0) * jnp.sin(qang)

    gate = max(NX - 2, 0)

    @pl.when(strand == FIRST)
    def _():
        for i in range(len(hp)):
            x_copy(i, gate).wait_send()
        pl.semaphore_signal(turn, inc=1, device_id={"strand": other_strand}, device_id_type=MESH)

    @pl.when(strand != FIRST)
    def _():
        pl.semaphore_wait(turn, 1)
        for c in range(NX):
            for i in range(len(hp)):
                x_copy(i, c).start()


    for k in (1, 2, 3, 7, 8, 9):
        loads[k].wait()
    kv_sum = jnp.zeros((kvl, rows), F32)
    q_sum = jnp.zeros((rows, lh * KDIM), F32)
    total_square = jnp.zeros((rows, 1), F32)
    for peer in [h] + hp:
        for c in range(NX):
            if peer is not h:
                pltpu.make_async_remote_copy(
                    xbuf.at[peer, c], xbuf.at[peer, c], xs.at[0, c], xr.at[peer, c],
                    device_id={"heads": peer}, device_id_type=MESH,
                ).wait_recv()
            piece = xbuf[peer, c].astype(F32)
            total_square = total_square + jnp.sum(piece * piece, axis=1, keepdims=True)
            first = peer * dl + c * xw
            gain = jnp.concatenate(
                [g1_ref[pl.ds(first // 128 + j, 1), :] for j in range(xw // 128)], axis=1
            )
            gained = (piece * gain).astype(BF16)
            at = pl.ds(pl.multiple_of(first, 128), xw)
            kv_sum = kv_sum + lax.dot_general(wkv[:, at], gained, NT, preferred_element_type=F32)
            if peer is hp[-1] and c == NX - 1:
                break
            q_sum = q_sum + jnp.dot(gained, wq[at, :], preferred_element_type=F32)
    scale = lax.rsqrt(total_square / D + 1e-06)
    scale_row = jnp.transpose(jnp.broadcast_to(scale, (rows, 128)))[:1, :]
    kvbuf[z, h] = (kv_sum * scale_row).astype(BF16)

    def kv_copy(p, hh, send, target):
        return pltpu.make_async_remote_copy(
            kvbuf.at[p, hh], kvbuf.at[p, hh], send, kvr.at[p, hh],
            device_id=target, device_id_type=MESH,
        )

    @pl.when(z < N - 1)
    def _():
        pl.semaphore_wait(ready, (N - 1 - z) * H)

    for i in range(N - 1):
        p = farthest(z, i, N)
        cp = kv_copy(z, h, kvs.at[i], {"pos": p})
        cp.start()
        sends.append(cp)

        @pl.when(direct(p))
        def _():
            for j, other in enumerate(hp):
                kv_copy(z, h, kds.at[j, i], {"pos": p, "heads": other}).start()

        if i > 0:
            continue
        for j, other in enumerate(hp):
            cp = kv_copy(z, h, kfs.at[j, 0], {"heads": other})
            cp.start()
            sends.append(cp)

    q_sum = q_sum + jnp.dot(gained, wq[at, :], preferred_element_type=F32)
    queries = (q_sum * scale).astype(BF16).astype(F32)
    rotated = []
    for a in range(lh):
        qa = queries[:, a * KDIM : (a + 1) * KDIM]
        rotated.append((qa * qcos + pltpu.roll(qa, half, 1) * qsin).astype(BF16))

    @pl.when(strand == FIRST)
    def _():
        for j, other in enumerate(hp):
            kv_copy(z, other, kfs.at[j, 0], {"heads": other}).wait_recv()
            for i, peer in enumerate(zp):
                @pl.when(jnp.logical_not(direct(peer)))
                def _():
                    kv_copy(z, other, kfs.at[j, i + 1], {"pos": peer}).start()

    loads[5].wait()
    for i in range(0, D, 128):
        wt[:, i : i + 128, :] = jnp.swapaxes(wraw[i : i + 128], 0, 1)
    score_parts, vts = [[] for _ in range(lh)], []
    for p in [z] + zp:
        if p is not z:
            kv_copy(p, h, kvs.at[0], {"pos": p}).wait_recv()
            for other in hp:
                kv_copy(p, other, kfs.at[0, 0], {"heads": other}).wait_recv()
        else:
            @pl.when(strand != FIRST)
            def _():
                for other in hp:
                    kv_copy(z, other, kfs.at[0, 0], {"heads": other}).wait_recv()
        kt = jnp.concatenate([kvbuf[p, i, :kl, :] for i in range(H)], axis=0).astype(F32)
        lo, hi = kt[:half], kt[half:]
        kt = jnp.concatenate(
            [lo * tabc[p] - hi * tabs[p], hi * tabc[p] + lo * tabs[p]], axis=0
        ).astype(BF16)
        vts.append(jnp.concatenate([kvbuf[p, i, kl:, :] for i in range(H)], axis=0))
        for a in range(lh):
            score_parts[a].append(
                jnp.dot(rotated[a], kt, preferred_element_type=F32) * KDIM ** (-0.5)
            )
    vt = jnp.concatenate(vts, axis=1)
    x = jnp.concatenate([xbuf[i, c] for i in range(H) for c in range(NX)], axis=1)
    heads_out = []
    for a in range(lh):
        scores = jnp.concatenate(score_parts[a], axis=1)
        top = jnp.max(scores, axis=1, keepdims=True)
        weights = jnp.exp(scores - top)
        weight_sum = jnp.sum(weights, axis=1, keepdims=True)
        mixed = lax.dot_general(weights.astype(BF16), vt, NT, preferred_element_type=F32)
        heads_out.append(mixed / weight_sum)
    merged = jnp.concatenate(heads_out, axis=1).astype(BF16)

    loads[4].wait()
    cw = D // NC
    for c in range(NC):
        part = jnp.dot(merged, wo[:, c * cw : (c + 1) * cw], preferred_element_type=F32)
        own[c] = part
        psend[c] = part.astype(BF16)
        for i, peer in enumerate(hp):
            cp = pltpu.make_async_remote_copy(
                psend.at[c], precv.at[h, c], ps.at[i, c], pr.at[h, c],
                device_id={"heads": peer}, device_id_type=MESH,
            )
            cp.start()
            sends.append(cp)
    hr = rows // 2
    swaps = []
    square = jnp.zeros((rows, 1), F32)
    for c in range(NC):
        summed = x[:, c * cw : (c + 1) * cw].astype(F32) + own[c]
        for peer in hp:
            pltpu.make_async_remote_copy(
                psend.at[c], precv.at[peer, c], ps.at[0, c], pr.at[peer, c],
                device_id={"heads": peer}, device_id_type=MESH,
            ).wait_recv()
            summed = summed + precv[peer, c].astype(F32)
        hidden = summed.astype(BF16).astype(F32)
        square = square + jnp.sum(hidden * hidden, axis=1, keepdims=True)
        gained = (hidden * spread(g2_ref[...], c * cw // 128, cw // 128)).astype(BF16)
        last = c == NC - 1
        for s in (other_strand, strand):
            part = jnp.dot(gained, wt[s, c * cw : (c + 1) * cw, :], preferred_element_type=F32)
            if c > 0:
                part = lg[s] + part
            if not last:
                lg[s] = part
                continue
            logits = part * lax.rsqrt(square / D + 1e-06)
            for r in range(2):
                part = logits[r * hr : (r + 1) * hr]
                track = (jnp.maximum(part, 0.0) + jnp.log1p(jnp.exp(-jnp.abs(part)))).astype(BF16)
                if s is strand:
                    out_ref[strand, r * hr : (r + 1) * hr, :] = track
                    continue
                snd[r] = track
                cp = pltpu.make_async_remote_copy(
                    snd.at[r], rcv.at[r], ss.at[r], sr.at[r],
                    device_id={"strand": other_strand}, device_id_type=MESH,
                )
                cp.start()
                sends.append(cp)
                swaps.append(cp)
    for r in range(2):
        swaps[r].wait_recv()
        out_ref[other_strand, r * hr : (r + 1) * hr, :] = rcv[r]
    for cp in sends:
        cp.wait_send()
    for i in range(len(hp)):
        for c in range(NX):
            if c != gate:
                x_copy(i, c).wait_send()

        @pl.when(strand != FIRST)
        def _():
            x_copy(i, gate).wait_send()

        for j in range(N - 1):
            p = farthest(z, j, N)

            @pl.when(direct(p))
            def _():
                kv_copy(z, h, kds.at[i, j], {"pos": p, "heads": hp[i]}).wait_send()

        for j, peer in enumerate(zp):
            @pl.when(jnp.logical_not(direct(peer)))
            def _():
                kv_copy(z, hp[i], kfs.at[i, j + 1], {"pos": peer}).wait_send()


def average(H, tracks_ref, tp_ref, out_ref):
    cols = out_ref.shape[1]
    pairs = tp_ref[...]
    first = (lax.axis_index("strand") * H + lax.axis_index("heads")) * cols
    lane = lax.broadcasted_iota(jnp.int32, (1, 128), 1)
    for b in range(cols // 128):
        at = slice(b * 128, (b + 1) * 128)
        r = tracks_ref[1, :, at].astype(F32)
        crossed = jnp.where(lane % 2 == 0, pltpu.roll(r, 127, 1), pltpu.roll(r, 1, 1))
        stays = pairs[b : b + 1, :] == first + b * 128 + lane
        r = jnp.where(stays, r, crossed)
        out_ref[:, at] = 0.5 * (tracks_ref[0, :, at].astype(F32) + r)


def body(
    base_codes, embed_table, attn_gain, w_query, w_key, w_value, w_out, head_gain, w_tracks, track_pairs
):
    H = lax.axis_size("heads")
    N = lax.axis_size("pos")
    rows = base_codes.shape[0] // BIN
    dl = embed_table.shape[1]
    D = dl * H
    cols = w_tracks.shape[2]
    kvl = w_key.shape[1] + w_value.shape[1]
    NC, NX = 6, 3
    vm = pl.BlockSpec(memory_space=pltpu.VMEM)
    hbm = pl.BlockSpec(memory_space=pl.ANY)
    dma = pltpu.SemaphoreType.DMA
    hm = max(H - 1, 1)
    zm = max(N - 1, 1)
    tracks, pairs = pl.pallas_call(
        functools.partial(kernel, H, N, NC, NX),
        out_shape=[pltpu.VMEM((2, rows, cols), BF16), pltpu.VMEM((cols // 128, 128), jnp.int32)],
        in_specs=[hbm] * 10,
        out_specs=[vm, vm],
        scratch_shapes=[
            pltpu.VMEM((rows, BIN), jnp.int32),
            pltpu.VMEM((D // 128, 128), F32),
            pltpu.VMEM((D // 128, 128), F32),
            pltpu.VMEM(embed_table.shape, BF16),
            pltpu.VMEM(w_query.shape, BF16),
            pltpu.VMEM((kvl, D), BF16),
            pltpu.VMEM(w_out.shape, BF16),
            pltpu.VMEM(w_tracks.shape, BF16),
            pltpu.VMEM((2, D, cols), BF16),
            pltpu.VMEM((H, NX, rows, dl // NX), BF16),
            pltpu.VMEM((N, H, kvl, rows), BF16),
            pltpu.VMEM((N, KDIM // 2, rows), F32),
            pltpu.VMEM((N, KDIM // 2, rows), F32),
            pltpu.VMEM((NC, rows, D // NC), F32),
            pltpu.VMEM((NC, rows, D // NC), BF16),
            pltpu.VMEM((H, NC, rows, D // NC), BF16),
            pltpu.VMEM((2, rows, cols), F32),
            pltpu.VMEM((2, rows // 2, cols), BF16),
            pltpu.VMEM((2, rows // 2, cols), BF16),
            dma((10,)),
            dma((hm, NX)),
            dma((H, NX)),
            dma((zm,)),
            dma((N, H)),
            dma((hm, N)),
            dma((hm, zm)),
            dma((hm, NC)),
            dma((H, NC)),
            dma((2,)),
            dma((2,)),
            pltpu.SemaphoreType.REGULAR,
            pltpu.SemaphoreType.REGULAR,
        ],
        compiler_params=pltpu.CompilerParams(
            collective_id=0, has_side_effects=True, vmem_limit_bytes=60 * 1024 * 1024
        ),
    )(
        base_codes.reshape(rows, BIN),
        embed_table,
        attn_gain.reshape(D // 128, 128),
        w_query,
        w_key.T,
        w_value.T,
        w_out,
        head_gain.reshape(D // 128, 128),
        w_tracks,
        track_pairs.reshape(cols // 128, 128),
    )
    keep = pltpu.with_memory_space_constraint
    return pl.pallas_call(
        functools.partial(average, H),
        out_shape=jax.ShapeDtypeStruct((rows, cols), F32),
        in_specs=[vm, vm],
        out_specs=vm,
    )(keep(tracks, pltpu.VMEM), keep(pairs, pltpu.VMEM))


def solution(mesh):
    placed = (
        P(("groups", "pos")),
        P(None, "heads"),
        P(),
        P(None, "heads"),
        P(None, "heads"),
        P(None, "heads"),
        P("heads", None),
        P(),
        P(None, None, "heads"),
        P(("strand", "heads")),
    )
    return jax.shard_map(
        body,
        mesh=mesh,
        in_specs=placed,
        out_specs=P(("groups", "pos"), ("strand", "heads")),
        check_vma=False,
    )
```

```python
import functools
import math

import jax
import jax.numpy as jnp
from jax import lax
from jax.experimental import pallas as pl
from jax.experimental.pallas import tpu as pltpu
from jax.sharding import PartitionSpec as P

KDIM = 128
VDIM = 192
BIN = 128
F32 = jnp.float32
BF16 = jnp.bfloat16
MESH = pl.DeviceIdType.MESH
NT = (((1,), (1,)), ((), ()))
FIRST = 1
GROUPS = (2, 4, 4, 2)
PARTS = 4


def spread(table, first, count):
    return jnp.concatenate([table[first + i : first + i + 1, :] for i in range(count)], axis=1)


def partner(z, step, N):
    if N & (N - 1):
        return lax.rem(z + step, N)
    bit = 1
    while bit < N:
        if step & bit:
            z = z + bit - 2 * bit * ((z // bit) % 2)
        bit *= 2
    return z


def farthest(z, k, N):
    up = (N - 1 - z - k + N - 1) // N
    return up * (N - 1 - k) + (1 - up) * (k + z - (N - 1))


def kernel(
    H, N, NC, NX,
    codes_hbm, et_hbm, g1_hbm, wq_hbm, wk_hbm, wv_hbm, wo_hbm, g2_hbm, wt_hbm, tp_hbm,
    out_ref,
    tp_ref, codes_ref, gains, et, wq, wkv, wo, wraw, wt, xbuf, kvbuf, tabc, tabs, own, psend, precv, lg, snd, rcv,
    ls, xs, xr, kvs, kvr, ss, sr, ready, turn,
):
    h = lax.axis_index("heads")
    z = lax.axis_index("pos")
    strand = lax.axis_index("strand")
    rows = codes_hbm.shape[0]
    dl = et.shape[1]
    D = dl * H
    kl = wk_hbm.shape[0]
    kvl = wkv.shape[0]
    lh = wq.shape[1] // KDIM
    cols = wt.shape[2]
    total = rows * N

    hp = [lax.rem(h + i, H) for i in range(1, H)]
    zp = [partner(z, i, N) for i in range(1, N)]
    other_strand = 1 - strand

    def direct(p):
        return (4 * p < N) | (2 * (z - p) >= N)

    barrier = pltpu.get_barrier_semaphore()

    def greet(sem, up):
        for peer in zp:
            @pl.when(peer > z if up else peer < z)
            def _():
                for other in [h] + hp:
                    pl.semaphore_signal(
                        sem, inc=1, device_id={"pos": peer, "heads": other}, device_id_type=MESH
                    )

    greet(barrier, True)
    for peer in hp:
        pl.semaphore_signal(barrier, inc=1, device_id={"heads": peer}, device_id_type=MESH)
    pl.semaphore_signal(barrier, inc=1, device_id={"strand": other_strand}, device_id_type=MESH)

    xw = dl // NX
    load_codes = pltpu.make_async_copy(codes_hbm, codes_ref, ls.at[0])
    load_wq = pltpu.make_async_copy(wq_hbm, wq, ls.at[0])
    load_et = [
        pltpu.make_async_copy(
            et_hbm.at[:, pl.ds(c * xw, xw)], et.at[:, pl.ds(c * xw, xw)], ls.at[1 + c]
        )
        for c in range(NX)
    ]
    load_tp = pltpu.make_async_copy(tp_hbm, tp_ref, ls.at[1])
    load_wt = pltpu.make_async_copy(wt_hbm, wraw, ls.at[2])
    load_wo = pltpu.make_async_copy(wo_hbm, wo, ls.at[3])
    load_codes.start()
    for cp in load_et:
        cp.start()
    pltpu.make_async_copy(g1_hbm, gains.at[0], ls.at[1 + NX]).start()
    pltpu.make_async_copy(g2_hbm, gains.at[1], ls.at[1 + NX]).start()

    fwd = strand == 0
    width = 4 * BIN
    src_row = lax.broadcasted_iota(jnp.int32, (BIN, width), 0)
    place = lax.broadcasted_iota(jnp.int32, (BIN, width), 1) // 4
    want = jnp.where(fwd, place, BIN - 1 - place)
    expand = (src_row == want).astype(F32).astype(BF16)
    load_codes.wait()
    repeated = jnp.dot(codes_ref[...].astype(F32).astype(BF16), expand, preferred_element_type=F32)
    letter = lax.broadcasted_iota(jnp.int32, (rows, width), 1) % 4
    letter = jnp.where(fwd, letter, 3 - letter).astype(F32)
    onehot = (repeated == letter).astype(F32).astype(BF16)

    pltpu.make_async_copy(wk_hbm, wkv.at[pl.ds(0, kl), :], ls.at[2 + NX]).start()
    pltpu.make_async_copy(wv_hbm, wkv.at[pl.ds(kl, kvl - kl), :], ls.at[2 + NX]).start()
    load_wq.start()
    gate = max(NX - 2, 0)

    def x_copy(i, c):
        return pltpu.make_async_remote_copy(
            xbuf.at[h, c], xbuf.at[h, c], xs.at[int(c > gate)], xr.at[H - 2 - i, int(c > gate)],
            device_id={"heads": hp[i]}, device_id_type=MESH,
        )

    def x_wait(part, i, count, first):
        chunks = pl.ds(0, gate + 1) if part == 0 else pl.ds(gate + 1, NX - 1 - gate)
        ref = xbuf.at[pl.ds(first, count), chunks]
        return pltpu.make_async_remote_copy(
            ref, ref, xs.at[part], xr.at[i, part], device_id={"heads": hp[i]}, device_id_type=MESH
        )

    for c in range(NX):
        load_et[c].wait()
        part = jnp.dot(onehot, et[:, c * xw : (c + 1) * xw], preferred_element_type=F32)
        xbuf[h, c] = part.astype(BF16)
        if c == 0:
            pl.semaphore_wait(barrier, len(hp) + 1 + z * H)
            greet(ready, False)

        @pl.when(strand == FIRST)
        def _():
            for i in range(len(hp)):
                x_copy(i, c).start()
    load_wt.start()
    load_wo.start()
    load_tp.start()

    half = KDIM // 2
    step = -math.log(10000.0) / half
    lane_pos = lax.broadcasted_iota(jnp.int32, (half, rows), 1)
    kinv = jnp.exp(lax.broadcasted_iota(jnp.int32, (half, rows), 0).astype(F32) * step)
    for p in range(N):
        pos = lane_pos + p * rows
        pos = jnp.where(fwd, pos, total - 1 - pos).astype(F32)
        tabc[p] = jnp.cos(pos * kinv)
        tabs[p] = jnp.sin(pos * kinv)
    qpos = lax.broadcasted_iota(jnp.int32, (rows, KDIM), 0) + z * rows
    qpos = jnp.where(fwd, qpos, total - 1 - qpos).astype(F32)
    qlane = lax.broadcasted_iota(jnp.int32, (rows, KDIM), 1)
    qang = qpos * jnp.exp((qlane % half).astype(F32) * step)
    qcos = jnp.cos(qang)
    qsin = jnp.where(qlane < half, -1.0, 1.0) * jnp.sin(qang)


    @pl.when(strand == FIRST)
    def _():
        x_wait(0, 0, H - 1, 0).wait_send()
        pl.semaphore_signal(turn, inc=1, device_id={"strand": other_strand}, device_id_type=MESH)

    @pl.when(strand != FIRST)
    def _():
        pl.semaphore_wait(turn, 1)
        for c in range(NX):
            for i in range(len(hp)):
                x_copy(i, c).start()


    pltpu.make_async_copy(gains, gains, ls.at[1 + NX]).wait()
    pltpu.make_async_copy(wkv, wkv, ls.at[2 + NX]).wait()
    load_wq.wait()
    kv_sum = jnp.zeros((kvl, rows), F32)
    q_sum = jnp.zeros((rows, lh * KDIM), F32)
    total_square = jnp.zeros((rows, 1), F32)
    for k, peer in enumerate([h] + hp):
        for c in range(NX):
            if k > 0 and c in (0, gate + 1):
                x_wait(int(c > gate), k - 1, 1, peer).wait_recv()
            piece = xbuf[peer, c].astype(F32)
            total_square = total_square + jnp.sum(piece * piece, axis=1, keepdims=True)
            first = peer * dl + c * xw
            gain = jnp.concatenate(
                [gains[0, pl.ds(first // 128 + j, 1), :] for j in range(xw // 128)], axis=1
            )
            gained = (piece * gain).astype(BF16)
            at = pl.ds(pl.multiple_of(first, 128), xw)
            kv_sum = kv_sum + lax.dot_general(wkv[:, at], gained, NT, preferred_element_type=F32)
            if peer is hp[-1] and c == NX - 1:
                break
            q_sum = q_sum + jnp.dot(gained, wq[at, :], preferred_element_type=F32)
    scale = lax.rsqrt(total_square / D + 1e-06)
    scale_row = jnp.transpose(jnp.broadcast_to(scale, (rows, 128)))[:1, :]
    kvbuf[z, h] = (kv_sum * scale_row).astype(BF16)

    def kv_copy(p, hh, send, target):
        return pltpu.make_async_remote_copy(
            kvbuf.at[p, hh], kvbuf.at[p, hh], send, kvr.at[p],
            device_id=target, device_id_type=MESH,
        )

    def kv_wait(ref, send, p):
        return pltpu.make_async_remote_copy(
            ref, ref, send, kvr.at[p], device_id={"heads": hp[0]}, device_id_type=MESH
        )

    @pl.when(z < N - 1)
    def _():
        pl.semaphore_wait(ready, (N - 1 - z) * H)

    for j, other in enumerate(hp):
        kv_copy(z, h, ss, {"heads": other}).start()
    for i in range(N - 1):
        p = farthest(z, i, N)
        kv_copy(z, h, kvs, {"pos": p}).start()

        @pl.when(direct(p))
        def _():
            for j, other in enumerate(hp):
                kv_copy(z, h, kvs, {"pos": p, "heads": other}).start()

    q_sum = q_sum + jnp.dot(gained, wq[at, :], preferred_element_type=F32)
    queries = (q_sum * scale).astype(BF16).astype(F32)
    rotated = []
    for a in range(lh):
        qa = queries[:, a * KDIM : (a + 1) * KDIM]
        rotated.append((qa * qcos + pltpu.roll(qa, half, 1) * qsin).astype(BF16))

    kv_wait(kvbuf.at[z, pl.ds(0, H - 1)], ss, z).wait_recv()
    for peer in zp:
        @pl.when(jnp.logical_not(direct(peer)))
        def _():
            for other in hp:
                kv_copy(z, other, kvs, {"pos": peer}).start()

    load_wt.wait()
    for i in range(0, D, 128):
        wt[:, i : i + 128, :] = jnp.swapaxes(wraw[i : i + 128], 0, 1)
    score_parts, vts = [[] for _ in range(lh)], []
    for p in [z] + zp:
        if p is not z:
            kv_wait(kvbuf.at[p], kvs, p).wait_recv()
        kt = jnp.concatenate([kvbuf[p, i, :kl, :] for i in range(H)], axis=0).astype(F32)
        lo, hi = kt[:half], kt[half:]
        kt = jnp.concatenate(
            [lo * tabc[p] - hi * tabs[p], hi * tabc[p] + lo * tabs[p]], axis=0
        ).astype(BF16)
        vts.append(jnp.concatenate([kvbuf[p, i, kl:, :] for i in range(H)], axis=0))
        for a in range(lh):
            score_parts[a].append(
                jnp.dot(rotated[a], kt, preferred_element_type=F32) * KDIM ** (-0.5)
            )
    vt = jnp.concatenate(vts, axis=1)
    x = jnp.concatenate([xbuf[i, c] for i in range(H) for c in range(NX)], axis=1)
    heads_out = []
    for a in range(lh):
        scores = jnp.concatenate(score_parts[a], axis=1)
        top = jnp.max(scores, axis=1, keepdims=True)
        weights = jnp.exp(scores - top)
        weight_sum = jnp.sum(weights, axis=1, keepdims=True)
        mixed = lax.dot_general(weights.astype(BF16), vt, NT, preferred_element_type=F32)
        heads_out.append(mixed / weight_sum)
    merged = jnp.concatenate(heads_out, axis=1).astype(BF16)

    load_wo.wait()
    uw = D // sum(GROUPS)
    edges = [sum(GROUPS[:c]) for c in range(NC + 1)]

    def part_copy(c, i, owner, slot):
        units = pl.ds(edges[c], GROUPS[c])
        return pltpu.make_async_remote_copy(
            psend.at[units], precv.at[owner, units], xs.at[0], xr.at[slot, c],
            device_id={"heads": hp[i]}, device_id_type=MESH,
        )

    @pl.when(strand != FIRST)
    def _():
        x_wait(0, 0, H - 1, 0).wait_send()

    for c in range(NC):
        lo, hi = edges[c] * uw, edges[c + 1] * uw
        part = jnp.dot(merged, wo[:, lo:hi], preferred_element_type=F32)
        rounded = part.astype(BF16)
        for u in range(GROUPS[c]):
            psend[edges[c] + u] = rounded[:, u * uw : (u + 1) * uw]
        for i in range(len(hp)):
            part_copy(c, i, h, H - 2 - i).start()
        own[:, lo:hi] = x[:, lo:hi].astype(F32) + part
    x_wait(1, 0, H - 1, 0).wait_send()
    kv_wait(kvbuf.at[z, pl.ds(0, H - 1)], ss, z).wait_send()
    kv_wait(kvbuf.at[pl.ds(0, N - 1)], kvs, z).wait_send()
    load_tp.wait()
    hr = rows // 2
    swaps = []
    square = jnp.zeros((rows, 1), F32)
    blocks = cols // 128
    lane = lax.broadcasted_iota(jnp.int32, (1, 128), 1)
    stays = [
        tp_ref[b : b + 1, :] == (strand * H + h) * cols + b * 128 + lane for b in range(blocks)
    ]

    def cross(values, b, forward):
        swapped = jnp.where(lane % 2 == 0, pltpu.roll(values, 127, 1), pltpu.roll(values, 1, 1))
        return jnp.where(stays[b] | forward, values, swapped)

    for c in range(NC):
        a, e = edges[c] * uw, edges[c + 1] * uw
        summed = own[:, a:e]
        for i, peer in enumerate(hp):
            part_copy(c, i, peer, i).wait_recv()
            summed = summed + jnp.concatenate(
                [precv[peer, u].astype(F32) for u in range(edges[c], edges[c + 1])], axis=1
            )
        hidden = summed.astype(BF16).astype(F32)
        square = square + jnp.sum(hidden * hidden, axis=1, keepdims=True)
        gained = (hidden * spread(gains[1], a // 128, (e - a) // 128)).astype(BF16)
        last = c == NC - 1
        for s in (other_strand, strand):
            part = jnp.dot(gained, wt[s, a:e, :], preferred_element_type=F32)
            if c > 0:
                part = lg[s] + part
            if not last:
                lg[s] = part
                continue
            logits = part * lax.rsqrt(square / D + 1e-06)
            for r in range(2):
                part = logits[r * hr : (r + 1) * hr]
                track = (jnp.maximum(part, 0.0) + jnp.log1p(jnp.exp(-jnp.abs(part)))).astype(BF16)
                if s is strand:
                    for b in range(blocks):
                        at = slice(b * 128, (b + 1) * 128)
                        out_ref[r * hr : (r + 1) * hr, at] = 0.5 * cross(
                            track[:, at].astype(F32), b, fwd
                        )
                    continue
                snd[r] = track
                cp = pltpu.make_async_remote_copy(
                    snd.at[r], rcv.at[r], ss, sr.at[r],
                    device_id={"strand": other_strand}, device_id_type=MESH,
                )
                cp.start()
                swaps.append(cp)
    sent = precv.at[pl.ds(0, H - 1)]
    pltpu.make_async_remote_copy(
        sent, sent, xs.at[0], xr.at[0, 0], device_id={"heads": hp[0]}, device_id_type=MESH
    ).wait_send()
    for r in range(2):
        swaps[r].wait_recv()
        for b in range(blocks):
            at = slice(b * 128, (b + 1) * 128)
            rr = slice(r * hr, (r + 1) * hr)
            out_ref[rr, at] = out_ref[rr, at] + 0.5 * cross(
                rcv[r, :, at].astype(F32), b, jnp.logical_not(fwd)
            )
    pltpu.make_async_remote_copy(
        snd, rcv, ss, sr.at[0], device_id={"strand": other_strand}, device_id_type=MESH
    ).wait_send()


def store(src_ref, out_ref, sem):
    rows = src_ref.shape[0]
    step = rows // PARTS
    copies = [
        pltpu.make_async_copy(
            src_ref.at[pl.ds(i * step, step)], out_ref.at[pl.ds(i * step, step)], sem.at[i]
        )
        for i in range(PARTS)
    ]
    for cp in copies:
        cp.start()
    for cp in copies:
        cp.wait()


def body(
    base_codes, embed_table, attn_gain, w_query, w_key, w_value, w_out, head_gain, w_tracks, track_pairs
):
    H = lax.axis_size("heads")
    N = lax.axis_size("pos")
    rows = base_codes.shape[0] // BIN
    dl = embed_table.shape[1]
    D = dl * H
    cols = w_tracks.shape[2]
    kvl = w_key.shape[1] + w_value.shape[1]
    NC, NX = len(GROUPS), 3
    vm = pl.BlockSpec(memory_space=pltpu.VMEM)
    hbm = pl.BlockSpec(memory_space=pl.ANY)
    dma = pltpu.SemaphoreType.DMA
    hm = max(H - 1, 1)
    tracks = pl.pallas_call(
        functools.partial(kernel, H, N, NC, NX),
        out_shape=pltpu.VMEM((rows, cols), F32),
        in_specs=[hbm] * 10,
        out_specs=vm,
        scratch_shapes=[
            pltpu.VMEM((cols // 128, 128), jnp.int32),
            pltpu.VMEM((rows, BIN), jnp.int32),
            pltpu.VMEM((2, D // 128, 128), F32),
            pltpu.VMEM(embed_table.shape, BF16),
            pltpu.VMEM(w_query.shape, BF16),
            pltpu.VMEM((kvl, D), BF16),
            pltpu.VMEM(w_out.shape, BF16),
            pltpu.VMEM(w_tracks.shape, BF16),
            pltpu.VMEM((2, D, cols), BF16),
            pltpu.VMEM((H, NX, rows, dl // NX), BF16),
            pltpu.VMEM((N, H, kvl, rows), BF16),
            pltpu.VMEM((N, KDIM // 2, rows), F32),
            pltpu.VMEM((N, KDIM // 2, rows), F32),
            pltpu.VMEM((rows, D), F32),
            pltpu.VMEM((sum(GROUPS), rows, D // sum(GROUPS)), BF16),
            pltpu.VMEM((H, sum(GROUPS), rows, D // sum(GROUPS)), BF16),
            pltpu.VMEM((2, rows, cols), F32),
            pltpu.VMEM((2, rows // 2, cols), BF16),
            pltpu.VMEM((2, rows // 2, cols), BF16),
            dma((3 + NX,)),
            dma((2,)),
            dma((hm, NC)),
            dma,
            dma((N,)),
            dma,
            dma((2,)),
            pltpu.SemaphoreType.REGULAR,
            pltpu.SemaphoreType.REGULAR,
        ],
        compiler_params=pltpu.CompilerParams(
            collective_id=0, has_side_effects=True, vmem_limit_bytes=60 * 1024 * 1024
        ),
    )(
        base_codes.reshape(rows, BIN),
        embed_table,
        attn_gain.reshape(D // 128, 128),
        w_query,
        w_key.T,
        w_value.T,
        w_out,
        head_gain.reshape(D // 128, 128),
        w_tracks,
        track_pairs.reshape(cols // 128, 128),
    )
    return tracks


def solution(mesh):
    placed = (
        P(("groups", "pos")),
        P(None, "heads"),
        P(),
        P(None, "heads"),
        P(None, "heads"),
        P(None, "heads"),
        P("heads", None),
        P(),
        P(None, None, "heads"),
        P(("strand", "heads")),
    )
    return jax.shard_map(
        body,
        mesh=mesh,
        in_specs=placed,
        out_specs=P(("groups", "pos"), ("strand", "heads")),
        check_vma=False,
    )
```

```python
import functools
import math

import jax
import jax.numpy as jnp
from jax import lax
from jax.experimental import pallas as pl
from jax.experimental.pallas import tpu as pltpu
from jax.sharding import PartitionSpec as P

KDIM = 128
VDIM = 192
BIN = 128
F32 = jnp.float32
BF16 = jnp.bfloat16
MESH = pl.DeviceIdType.MESH
NT = (((1,), (1,)), ((), ()))
FIRST = 1
GROUPS = (2, 3, 3, 2, 2)
PARTS = 4


def spread(table, first, count):
    return jnp.concatenate([table[first + i : first + i + 1, :] for i in range(count)], axis=1)


def partner(z, step, N):
    if N & (N - 1):
        return lax.rem(z + step, N)
    bit = 1
    while bit < N:
        if step & bit:
            z = z + bit - 2 * bit * ((z // bit) % 2)
        bit *= 2
    return z


def farthest(z, k, N):
    up = (N - 1 - z - k + N - 1) // N
    return up * (N - 1 - k) + (1 - up) * (k + z - (N - 1))


def kernel(
    H, N, NC, NX,
    codes_hbm, et_hbm, g1_hbm, wq_hbm, wk_hbm, wv_hbm, wo_hbm, g2_hbm, wt_hbm, tp_hbm,
    out_ref,
    tp_ref, codes_ref, gains, et, wq, wkv, wo, wraw, wt, xbuf, kbuf, vbuf, tabc, tabs, own, psend, precv, lg, snd, rcv,
    ls, xs, xr, ks, vs, kr, vr, ss, sr, ready, turn,
):
    h = lax.axis_index("heads")
    z = lax.axis_index("pos")
    strand = lax.axis_index("strand")
    rows = codes_hbm.shape[0]
    dl = et.shape[1]
    D = dl * H
    kl = wk_hbm.shape[0]
    kvl = wkv.shape[0]
    lh = wq.shape[1] // KDIM
    cols = wt.shape[2]
    total = rows * N

    hp = [lax.rem(h + i, H) for i in range(1, H)]
    zp = [partner(z, i, N) for i in range(1, N)]
    other_strand = 1 - strand

    def direct(p):
        return (4 * p < N) | (2 * (z - p) >= N)

    barrier = pltpu.get_barrier_semaphore()

    def greet(sem, up):
        for peer in zp:
            @pl.when(peer > z if up else peer < z)
            def _():
                for other in [h] + hp:
                    pl.semaphore_signal(
                        sem, inc=1, device_id={"pos": peer, "heads": other}, device_id_type=MESH
                    )

    greet(barrier, True)
    for peer in hp:
        pl.semaphore_signal(barrier, inc=1, device_id={"heads": peer}, device_id_type=MESH)
    pl.semaphore_signal(barrier, inc=1, device_id={"strand": other_strand}, device_id_type=MESH)

    xw = dl // NX
    load_codes = pltpu.make_async_copy(codes_hbm, codes_ref, ls.at[0])
    load_wq = pltpu.make_async_copy(wq_hbm, wq, ls.at[0])
    load_et = [
        pltpu.make_async_copy(
            et_hbm.at[:, pl.ds(c * xw, xw)], et.at[:, pl.ds(c * xw, xw)], ls.at[1 + c]
        )
        for c in range(NX)
    ]
    load_tp = pltpu.make_async_copy(tp_hbm, tp_ref, ls.at[1])
    load_wt = pltpu.make_async_copy(wt_hbm, wraw, ls.at[2])
    load_wo = pltpu.make_async_copy(wo_hbm, wo, ls.at[3])
    load_codes.start()
    for cp in load_et:
        cp.start()
    pltpu.make_async_copy(g1_hbm, gains.at[0], ls.at[1 + NX]).start()
    pltpu.make_async_copy(g2_hbm, gains.at[1], ls.at[1 + NX]).start()

    fwd = strand == 0
    width = 4 * BIN
    src_row = lax.broadcasted_iota(jnp.int32, (BIN, width), 0)
    place = lax.broadcasted_iota(jnp.int32, (BIN, width), 1) // 4
    want = jnp.where(fwd, place, BIN - 1 - place)
    expand = (src_row == want).astype(F32).astype(BF16)
    load_codes.wait()
    repeated = jnp.dot(codes_ref[...].astype(F32).astype(BF16), expand, preferred_element_type=F32)
    letter = lax.broadcasted_iota(jnp.int32, (rows, width), 1) % 4
    letter = jnp.where(fwd, letter, 3 - letter).astype(F32)
    onehot = (repeated == letter).astype(F32).astype(BF16)

    pltpu.make_async_copy(wk_hbm, wkv.at[pl.ds(0, kl), :], ls.at[2 + NX]).start()
    pltpu.make_async_copy(wv_hbm, wkv.at[pl.ds(kl, kvl - kl), :], ls.at[2 + NX]).start()
    load_wq.start()
    gate = max(NX - 2, 0)

    def x_copy(i, c):
        return pltpu.make_async_remote_copy(
            xbuf.at[h, c], xbuf.at[h, c], xs.at[int(c > gate)], xr.at[H - 2 - i, int(c > gate)],
            device_id={"heads": hp[i]}, device_id_type=MESH,
        )

    def x_wait(part, i, count, first):
        chunks = pl.ds(0, gate + 1) if part == 0 else pl.ds(gate + 1, NX - 1 - gate)
        ref = xbuf.at[pl.ds(first, count), chunks]
        return pltpu.make_async_remote_copy(
            ref, ref, xs.at[part], xr.at[i, part], device_id={"heads": hp[i]}, device_id_type=MESH
        )

    for c in range(NX):
        load_et[c].wait()
        part = jnp.dot(onehot, et[:, c * xw : (c + 1) * xw], preferred_element_type=F32)
        xbuf[h, c] = part.astype(BF16)
        if c == 0:
            pl.semaphore_wait(barrier, len(hp) + 1 + z * H)
            greet(ready, False)

        @pl.when(strand == FIRST)
        def _():
            for i in range(len(hp)):
                x_copy(i, c).start()
    load_wt.start()
    load_wo.start()
    load_tp.start()

    half = KDIM // 2
    step = -math.log(10000.0) / half
    lane_pos = lax.broadcasted_iota(jnp.int32, (half, rows), 1)
    kinv = jnp.exp(lax.broadcasted_iota(jnp.int32, (half, rows), 0).astype(F32) * step)
    for p in range(N):
        pos = lane_pos + p * rows
        pos = jnp.where(fwd, pos, total - 1 - pos).astype(F32)
        tabc[p] = jnp.cos(pos * kinv)
        tabs[p] = jnp.sin(pos * kinv)
    qpos = lax.broadcasted_iota(jnp.int32, (rows, KDIM), 0) + z * rows
    qpos = jnp.where(fwd, qpos, total - 1 - qpos).astype(F32)
    qlane = lax.broadcasted_iota(jnp.int32, (rows, KDIM), 1)
    qang = qpos * jnp.exp((qlane % half).astype(F32) * step)
    qcos = jnp.cos(qang)
    qsin = jnp.where(qlane < half, -1.0, 1.0) * jnp.sin(qang)


    @pl.when(strand == FIRST)
    def _():
        x_wait(0, 0, H - 1, 0).wait_send()
        pl.semaphore_signal(turn, inc=1, device_id={"strand": other_strand}, device_id_type=MESH)

    @pl.when(strand != FIRST)
    def _():
        pl.semaphore_wait(turn, 1)
        for c in range(NX):
            for i in range(len(hp)):
                x_copy(i, c).start()


    pltpu.make_async_copy(gains, gains, ls.at[1 + NX]).wait()
    pltpu.make_async_copy(wkv, wkv, ls.at[2 + NX]).wait()
    load_wq.wait()
    kv_sum = jnp.zeros((kvl, rows), F32)
    q_sum = jnp.zeros((rows, lh * KDIM), F32)
    total_square = jnp.zeros((rows, 1), F32)
    for k, peer in enumerate([h] + hp):
        for c in range(NX):
            if k == 1 and c == 0:
                @pl.when(strand != FIRST)
                def _():
                    x_wait(0, 0, H - 1, 0).wait_send()

                x_wait(1, 0, H - 1, 0).wait_send()
            if k > 0 and c in (0, gate + 1):
                x_wait(int(c > gate), k - 1, 1, peer).wait_recv()
            piece = xbuf[peer, c].astype(F32)
            total_square = total_square + jnp.sum(piece * piece, axis=1, keepdims=True)
            first = peer * dl + c * xw
            gain = jnp.concatenate(
                [gains[0, pl.ds(first // 128 + j, 1), :] for j in range(xw // 128)], axis=1
            )
            gained = (piece * gain).astype(BF16)
            at = pl.ds(pl.multiple_of(first, 128), xw)
            kv_sum = kv_sum + lax.dot_general(wkv[:, at], gained, NT, preferred_element_type=F32)
            if peer is hp[-1] and c == NX - 1:
                break
            q_sum = q_sum + jnp.dot(gained, wq[at, :], preferred_element_type=F32)
    scale = lax.rsqrt(total_square / D + 1e-06)
    scale_row = jnp.transpose(jnp.broadcast_to(scale, (rows, 128)))[:1, :]
    kv_own = (kv_sum * scale_row).astype(BF16)
    kbuf[z, h] = kv_own[:kl]
    vbuf[z, h] = kv_own[kl:]
    parts = ((kbuf, ks, kr, xs.at[0]), (vbuf, vs, vr, xs.at[1]))

    def kv_copy(part, p, hh, send, target):
        buf, _, recv, _ = part
        return pltpu.make_async_remote_copy(
            buf.at[p, hh], buf.at[p, hh], send, recv.at[p], device_id=target, device_id_type=MESH
        )

    def kv_wait(part, ref, send, p):
        return pltpu.make_async_remote_copy(
            ref, ref, send, part[2].at[p], device_id={"heads": hp[0]}, device_id_type=MESH
        )

    @pl.when(z < N - 1)
    def _():
        pl.semaphore_wait(ready, (N - 1 - z) * H)

    for i in range(N - 1):
        p = farthest(z, i, N)
        for part in parts:
            kv_copy(part, z, h, part[1], {"pos": p}).start()

            @pl.when(direct(p))
            def _():
                for other in hp:
                    kv_copy(part, z, h, part[1], {"pos": p, "heads": other}).start()

            if i == 0:
                for other in hp:
                    kv_copy(part, z, h, part[3], {"heads": other}).start()

    q_sum = q_sum + jnp.dot(gained, wq[at, :], preferred_element_type=F32)
    queries = (q_sum * scale).astype(BF16).astype(F32)
    rotated = []
    for a in range(lh):
        qa = queries[:, a * KDIM : (a + 1) * KDIM]
        rotated.append((qa * qcos + pltpu.roll(qa, half, 1) * qsin).astype(BF16))

    for part in parts:
        kv_wait(part, part[0].at[z, pl.ds(0, H - 1)], part[3], z).wait_recv()
        for peer in zp:
            @pl.when(jnp.logical_not(direct(peer)))
            def _():
                for other in hp:
                    kv_copy(part, z, other, part[1], {"pos": peer}).start()

    load_wt.wait()
    for i in range(0, D, 128):
        wt[:, i : i + 128, :] = jnp.swapaxes(wraw[i : i + 128], 0, 1)
    score_parts, vts = [[] for _ in range(lh)], []
    for p in [z] + zp:
        if p is not z:
            kv_wait(parts[0], kbuf.at[p], ks, p).wait_recv()
        kt = jnp.concatenate([kbuf[p, i] for i in range(H)], axis=0).astype(F32)
        lo, hi = kt[:half], kt[half:]
        kt = jnp.concatenate(
            [lo * tabc[p] - hi * tabs[p], hi * tabc[p] + lo * tabs[p]], axis=0
        ).astype(BF16)
        for a in range(lh):
            score_parts[a].append(
                jnp.dot(rotated[a], kt, preferred_element_type=F32) * KDIM ** (-0.5)
            )
    for p in [z] + zp:
        if p is not z:
            kv_wait(parts[1], vbuf.at[p], vs, p).wait_recv()
        vts.append(jnp.concatenate([vbuf[p, i] for i in range(H)], axis=0))
    vt = jnp.concatenate(vts, axis=1)
    x = jnp.concatenate([xbuf[i, c] for i in range(H) for c in range(NX)], axis=1)
    heads_out = []
    for a in range(lh):
        scores = jnp.concatenate(score_parts[a], axis=1)
        top = jnp.max(scores, axis=1, keepdims=True)
        weights = jnp.exp(scores - top)
        weight_sum = jnp.sum(weights, axis=1, keepdims=True)
        mixed = lax.dot_general(weights.astype(BF16), vt, NT, preferred_element_type=F32)
        heads_out.append(mixed / weight_sum)
    merged = jnp.concatenate(heads_out, axis=1).astype(BF16)

    load_wo.wait()
    uw = D // sum(GROUPS)
    edges = [sum(GROUPS[:c]) for c in range(NC + 1)]

    def part_copy(c, i, owner, slot):
        units = pl.ds(edges[c], GROUPS[c])
        return pltpu.make_async_remote_copy(
            psend.at[units], precv.at[owner, units], xs.at[0], xr.at[slot, c],
            device_id={"heads": hp[i]}, device_id_type=MESH,
        )

    kv_wait(parts[0], kbuf.at[z, pl.ds(0, H - 1)], xs.at[0], z).wait_send()
    for c in range(NC):
        lo, hi = edges[c] * uw, edges[c + 1] * uw
        part = jnp.dot(merged, wo[:, lo:hi], preferred_element_type=F32)
        rounded = part.astype(BF16)
        for u in range(GROUPS[c]):
            psend[edges[c] + u] = rounded[:, u * uw : (u + 1) * uw]
        for i in range(len(hp)):
            part_copy(c, i, h, H - 2 - i).start()
        own[:, lo:hi] = x[:, lo:hi].astype(F32) + part
    kv_wait(parts[1], vbuf.at[z, pl.ds(0, H - 1)], xs.at[1], z).wait_send()
    for part in parts:
        kv_wait(part, part[0].at[pl.ds(0, N - 1)], part[1], z).wait_send()
    load_tp.wait()
    hr = rows // 2
    swaps = []
    square = jnp.zeros((rows, 1), F32)
    blocks = cols // 128
    lane = lax.broadcasted_iota(jnp.int32, (1, 128), 1)
    stays = [
        tp_ref[b : b + 1, :] == (strand * H + h) * cols + b * 128 + lane for b in range(blocks)
    ]

    def cross(values, b, forward):
        swapped = jnp.where(lane % 2 == 0, pltpu.roll(values, 127, 1), pltpu.roll(values, 1, 1))
        return jnp.where(stays[b] | forward, values, swapped)

    for c in range(NC):
        a, e = edges[c] * uw, edges[c + 1] * uw
        summed = own[:, a:e]
        for i, peer in enumerate(hp):
            part_copy(c, i, peer, i).wait_recv()
            summed = summed + jnp.concatenate(
                [precv[peer, u].astype(F32) for u in range(edges[c], edges[c + 1])], axis=1
            )
        hidden = summed.astype(BF16).astype(F32)
        square = square + jnp.sum(hidden * hidden, axis=1, keepdims=True)
        gained = (hidden * spread(gains[1], a // 128, (e - a) // 128)).astype(BF16)
        last = c == NC - 1
        for s in (other_strand, strand):
            part = jnp.dot(gained, wt[s, a:e, :], preferred_element_type=F32)
            if c > 0:
                part = lg[s] + part
            if not last:
                lg[s] = part
                continue
            logits = part * lax.rsqrt(square / D + 1e-06)
            for r in range(2):
                part = logits[r * hr : (r + 1) * hr]
                track = (jnp.maximum(part, 0.0) + jnp.log1p(jnp.exp(-jnp.abs(part)))).astype(BF16)
                if s is strand:
                    for b in range(blocks):
                        at = slice(b * 128, (b + 1) * 128)
                        out_ref[r * hr : (r + 1) * hr, at] = 0.5 * cross(
                            track[:, at].astype(F32), b, fwd
                        )
                    continue
                snd[r] = track
                cp = pltpu.make_async_remote_copy(
                    snd.at[r], rcv.at[r], ss, sr.at[r],
                    device_id={"strand": other_strand}, device_id_type=MESH,
                )
                cp.start()
                swaps.append(cp)
    sent = precv.at[pl.ds(0, H - 1)]
    pltpu.make_async_remote_copy(
        sent, sent, xs.at[0], xr.at[0, 0], device_id={"heads": hp[0]}, device_id_type=MESH
    ).wait_send()
    for r in range(2):
        swaps[r].wait_recv()
        for b in range(blocks):
            at = slice(b * 128, (b + 1) * 128)
            rr = slice(r * hr, (r + 1) * hr)
            out_ref[rr, at] = out_ref[rr, at] + 0.5 * cross(
                rcv[r, :, at].astype(F32), b, jnp.logical_not(fwd)
            )
    pltpu.make_async_remote_copy(
        snd, rcv, ss, sr.at[0], device_id={"strand": other_strand}, device_id_type=MESH
    ).wait_send()


def store(src_ref, out_ref, sem):
    rows = src_ref.shape[0]
    step = rows // PARTS
    copies = [
        pltpu.make_async_copy(
            src_ref.at[pl.ds(i * step, step)], out_ref.at[pl.ds(i * step, step)], sem.at[i]
        )
        for i in range(PARTS)
    ]
    for cp in copies:
        cp.start()
    for cp in copies:
        cp.wait()


def body(
    base_codes, embed_table, attn_gain, w_query, w_key, w_value, w_out, head_gain, w_tracks, track_pairs
):
    H = lax.axis_size("heads")
    N = lax.axis_size("pos")
    rows = base_codes.shape[0] // BIN
    dl = embed_table.shape[1]
    D = dl * H
    cols = w_tracks.shape[2]
    kvl = w_key.shape[1] + w_value.shape[1]
    NC, NX = len(GROUPS), 3
    vm = pl.BlockSpec(memory_space=pltpu.VMEM)
    hbm = pl.BlockSpec(memory_space=pl.ANY)
    dma = pltpu.SemaphoreType.DMA
    hm = max(H - 1, 1)
    tracks = pl.pallas_call(
        functools.partial(kernel, H, N, NC, NX),
        out_shape=pltpu.VMEM((rows, cols), F32),
        in_specs=[hbm] * 10,
        out_specs=vm,
        scratch_shapes=[
            pltpu.VMEM((cols // 128, 128), jnp.int32),
            pltpu.VMEM((rows, BIN), jnp.int32),
            pltpu.VMEM((2, D // 128, 128), F32),
            pltpu.VMEM(embed_table.shape, BF16),
            pltpu.VMEM(w_query.shape, BF16),
            pltpu.VMEM((kvl, D), BF16),
            pltpu.VMEM(w_out.shape, BF16),
            pltpu.VMEM(w_tracks.shape, BF16),
            pltpu.VMEM((2, D, cols), BF16),
            pltpu.VMEM((H, NX, rows, dl // NX), BF16),
            pltpu.VMEM((N, H, w_key.shape[1], rows), BF16),
            pltpu.VMEM((N, H, w_value.shape[1], rows), BF16),
            pltpu.VMEM((N, KDIM // 2, rows), F32),
            pltpu.VMEM((N, KDIM // 2, rows), F32),
            pltpu.VMEM((rows, D), F32),
            pltpu.VMEM((sum(GROUPS), rows, D // sum(GROUPS)), BF16),
            pltpu.VMEM((H, sum(GROUPS), rows, D // sum(GROUPS)), BF16),
            pltpu.VMEM((2, rows, cols), F32),
            pltpu.VMEM((2, rows // 2, cols), BF16),
            pltpu.VMEM((2, rows // 2, cols), BF16),
            dma((3 + NX,)),
            dma((2,)),
            dma((hm, NC)),
            dma,
            dma,
            dma((N,)),
            dma((N,)),
            dma,
            dma((2,)),
            pltpu.SemaphoreType.REGULAR,
            pltpu.SemaphoreType.REGULAR,
        ],
        compiler_params=pltpu.CompilerParams(
            collective_id=0, has_side_effects=True, vmem_limit_bytes=60 * 1024 * 1024
        ),
    )(
        base_codes.reshape(rows, BIN),
        embed_table,
        attn_gain.reshape(D // 128, 128),
        w_query,
        w_key.T,
        w_value.T,
        w_out,
        head_gain.reshape(D // 128, 128),
        w_tracks,
        track_pairs.reshape(cols // 128, 128),
    )
    return tracks


def solution(mesh):
    placed = (
        P(("groups", "pos")),
        P(None, "heads"),
        P(),
        P(None, "heads"),
        P(None, "heads"),
        P(None, "heads"),
        P("heads", None),
        P(),
        P(None, None, "heads"),
        P(("strand", "heads")),
    )
    return jax.shard_map(
        body,
        mesh=mesh,
        in_specs=placed,
        out_specs=P(("groups", "pos"), ("strand", "heads")),
        check_vma=False,
    )
```

```python
import functools
import math

import jax
import jax.numpy as jnp
from jax import lax
from jax.experimental import pallas as pl
from jax.experimental.pallas import tpu as pltpu
from jax.sharding import PartitionSpec as P

KDIM = 128
VDIM = 192
BIN = 128
F32 = jnp.float32
BF16 = jnp.bfloat16
MESH = pl.DeviceIdType.MESH
NT = (((1,), (1,)), ((), ()))
FIRST = 1
GROUPS = (2, 3, 3, 2, 2)
PARTS = 4


def spread(table, first, count):
    return jnp.concatenate([table[first + i : first + i + 1, :] for i in range(count)], axis=1)


def partner(z, step, N):
    if N & (N - 1):
        return lax.rem(z + step, N)
    bit = 1
    while bit < N:
        if step & bit:
            z = z + bit - 2 * bit * ((z // bit) % 2)
        bit *= 2
    return z


def farthest(z, k, N):
    up = (N - 1 - z - k + N - 1) // N
    return up * (N - 1 - k) + (1 - up) * (k + z - (N - 1))


def kernel(
    H, N, NC, NX,
    codes_hbm, et_hbm, g1_hbm, wq_hbm, wk_hbm, wv_hbm, wo_hbm, g2_hbm, wt_hbm, tp_hbm,
    out_ref,
    tp_ref, codes_ref, gains, et, wq, wkv, wo, wraw, wt, xbuf, kbuf, vbuf, tabc, tabs, own, psend, precv, lg, snd, rcv,
    ls, xs, xr, ks, vs, kr, vr, ss, sr, ready, turn,
):
    h = lax.axis_index("heads")
    z = lax.axis_index("pos")
    strand = lax.axis_index("strand")
    rows = codes_hbm.shape[0]
    dl = et.shape[1]
    D = dl * H
    kl = wk_hbm.shape[0]
    kvl = wkv.shape[0]
    lh = wq.shape[1] // KDIM
    cols = wt.shape[2]
    total = rows * N

    hp = [lax.rem(h + i, H) for i in range(1, H)]
    zp = [partner(z, i, N) for i in range(1, N)]
    other_strand = 1 - strand

    def direct(p):
        return (4 * p < N) | (2 * (z - p) >= N) | ((strand == FIRST) & (z - p == 1))

    barrier = pltpu.get_barrier_semaphore()

    def greet(sem, up):
        for peer in zp:
            @pl.when(peer > z if up else peer < z)
            def _():
                for other in [h] + hp:
                    pl.semaphore_signal(
                        sem, inc=1, device_id={"pos": peer, "heads": other}, device_id_type=MESH
                    )

    greet(barrier, True)
    for peer in hp:
        pl.semaphore_signal(barrier, inc=1, device_id={"heads": peer}, device_id_type=MESH)
    pl.semaphore_signal(barrier, inc=1, device_id={"strand": other_strand}, device_id_type=MESH)

    xunits = dl // 128
    lead = max(1, xunits // 3)
    after = max(1, xunits // 6)
    xsizes = (lead, after, xunits - lead - after)
    xat = [sum(xsizes[:c]) for c in range(NX + 1)]
    load_codes = pltpu.make_async_copy(codes_hbm, codes_ref, ls.at[0])
    load_wq = pltpu.make_async_copy(wq_hbm, wq, ls.at[0])
    load_et = [
        pltpu.make_async_copy(
            et_hbm.at[:, pl.ds(xat[c] * 128, xsizes[c] * 128)],
            et.at[:, pl.ds(xat[c] * 128, xsizes[c] * 128)],
            ls.at[1 + c],
        )
        for c in range(NX)
    ]
    load_tp = pltpu.make_async_copy(tp_hbm, tp_ref, ls.at[1])
    load_wt = pltpu.make_async_copy(wt_hbm, wraw, ls.at[2])
    load_wo = pltpu.make_async_copy(wo_hbm, wo, ls.at[3])
    load_codes.start()
    for cp in load_et:
        cp.start()
    pltpu.make_async_copy(g1_hbm, gains.at[0], ls.at[1 + NX]).start()
    pltpu.make_async_copy(g2_hbm, gains.at[1], ls.at[1 + NX]).start()

    fwd = strand == 0
    width = 4 * BIN
    src_row = lax.broadcasted_iota(jnp.int32, (BIN, width), 0)
    place = lax.broadcasted_iota(jnp.int32, (BIN, width), 1) // 4
    want = jnp.where(fwd, place, BIN - 1 - place)
    expand = (src_row == want).astype(F32).astype(BF16)
    load_codes.wait()
    repeated = jnp.dot(codes_ref[...].astype(F32).astype(BF16), expand, preferred_element_type=F32)
    letter = lax.broadcasted_iota(jnp.int32, (rows, width), 1) % 4
    letter = jnp.where(fwd, letter, 3 - letter).astype(F32)
    onehot = (repeated == letter).astype(F32).astype(BF16)

    pltpu.make_async_copy(wk_hbm, wkv.at[pl.ds(0, kl), :], ls.at[2 + NX]).start()
    pltpu.make_async_copy(wv_hbm, wkv.at[pl.ds(kl, kvl - kl), :], ls.at[2 + NX]).start()
    load_wq.start()
    gate = max(NX - 2, 0)

    def x_copy(i, c):
        ref = xbuf.at[h, pl.ds(xat[c], xsizes[c])]
        return pltpu.make_async_remote_copy(
            ref, ref, xs.at[int(c > gate)], xr.at[H - 2 - i, int(c > gate)],
            device_id={"heads": hp[i]}, device_id_type=MESH,
        )

    def x_wait(part, i, count, first):
        units = pl.ds(0, xat[gate + 1]) if part == 0 else pl.ds(xat[gate + 1], xat[NX] - xat[gate + 1])
        ref = xbuf.at[pl.ds(first, count), units]
        return pltpu.make_async_remote_copy(
            ref, ref, xs.at[part], xr.at[i, part], device_id={"heads": hp[i]}, device_id_type=MESH
        )

    for c in range(NX):
        load_et[c].wait()
        part = jnp.dot(
            onehot, et[:, xat[c] * 128 : xat[c + 1] * 128], preferred_element_type=F32
        ).astype(BF16)
        for u in range(xsizes[c]):
            xbuf[h, xat[c] + u] = part[:, u * 128 : (u + 1) * 128]
        if c == 0:
            pl.semaphore_wait(barrier, len(hp) + 1 + z * H)
            greet(ready, False)

        @pl.when(strand == FIRST)
        def _():
            for i in range(len(hp)):
                x_copy(i, c).start()
    load_wt.start()
    load_wo.start()
    load_tp.start()

    half = KDIM // 2
    step = -math.log(10000.0) / half
    lane_pos = lax.broadcasted_iota(jnp.int32, (half, rows), 1)
    kinv = jnp.exp(lax.broadcasted_iota(jnp.int32, (half, rows), 0).astype(F32) * step)
    for p in range(N):
        pos = lane_pos + p * rows
        pos = jnp.where(fwd, pos, total - 1 - pos).astype(F32)
        tabc[p] = jnp.cos(pos * kinv)
        tabs[p] = jnp.sin(pos * kinv)
    qpos = lax.broadcasted_iota(jnp.int32, (rows, KDIM), 0) + z * rows
    qpos = jnp.where(fwd, qpos, total - 1 - qpos).astype(F32)
    qlane = lax.broadcasted_iota(jnp.int32, (rows, KDIM), 1)
    qang = qpos * jnp.exp((qlane % half).astype(F32) * step)
    qcos = jnp.cos(qang)
    qsin = jnp.where(qlane < half, -1.0, 1.0) * jnp.sin(qang)


    @pl.when(strand == FIRST)
    def _():
        x_wait(0, 0, H - 1, 0).wait_send()
        pl.semaphore_signal(turn, inc=1, device_id={"strand": other_strand}, device_id_type=MESH)

    @pl.when(strand != FIRST)
    def _():
        pl.semaphore_wait(turn, 1)
        for c in range(NX):
            for i in range(len(hp)):
                x_copy(i, c).start()


    pltpu.make_async_copy(gains, gains, ls.at[1 + NX]).wait()
    pltpu.make_async_copy(wkv, wkv, ls.at[2 + NX]).wait()
    load_wq.wait()
    kv_sum = jnp.zeros((kvl, rows), F32)
    q_sum = jnp.zeros((rows, lh * KDIM), F32)
    total_square = jnp.zeros((rows, 1), F32)
    for k, peer in enumerate([h] + hp):
        for c in range(NX):
            if k == 1 and c == 0:
                @pl.when(strand != FIRST)
                def _():
                    x_wait(0, 0, H - 1, 0).wait_send()

                x_wait(1, 0, H - 1, 0).wait_send()
            if k > 0 and c in (0, gate + 1):
                x_wait(int(c > gate), k - 1, 1, peer).wait_recv()
            piece = jnp.concatenate(
                [xbuf[peer, u].astype(F32) for u in range(xat[c], xat[c + 1])], axis=1
            )
            total_square = total_square + jnp.sum(piece * piece, axis=1, keepdims=True)
            first = peer * dl + xat[c] * 128
            gain = jnp.concatenate(
                [gains[0, pl.ds(first // 128 + j, 1), :] for j in range(xsizes[c])], axis=1
            )
            gained = (piece * gain).astype(BF16)
            at = pl.ds(pl.multiple_of(first, 128), xsizes[c] * 128)
            kv_sum = kv_sum + lax.dot_general(wkv[:, at], gained, NT, preferred_element_type=F32)
            if peer is hp[-1] and c == NX - 1:
                break
            q_sum = q_sum + jnp.dot(gained, wq[at, :], preferred_element_type=F32)
    scale = lax.rsqrt(total_square / D + 1e-06)
    scale_row = jnp.transpose(jnp.broadcast_to(scale, (rows, 128)))[:1, :]
    kv_own = (kv_sum * scale_row).astype(BF16)
    kbuf[z, h] = kv_own[:kl]
    vbuf[z, h] = kv_own[kl:]
    parts = ((kbuf, ks, kr, xs.at[0]), (vbuf, vs, vr, xs.at[1]))

    def kv_copy(part, p, hh, send, target):
        buf, _, recv, _ = part
        return pltpu.make_async_remote_copy(
            buf.at[p, hh], buf.at[p, hh], send, recv.at[p], device_id=target, device_id_type=MESH
        )

    def kv_wait(part, ref, send, p):
        return pltpu.make_async_remote_copy(
            ref, ref, send, part[2].at[p], device_id={"heads": hp[0]}, device_id_type=MESH
        )

    @pl.when(z < N - 1)
    def _():
        pl.semaphore_wait(ready, (N - 1 - z) * H)

    for i in range(N - 1):
        p = farthest(z, i, N)

        @pl.when(direct(p))
        def _():
            for part in parts:
                for other in hp:
                    kv_copy(part, z, h, part[1], {"pos": p, "heads": other}).start()

        for part in parts:
            kv_copy(part, z, h, part[1], {"pos": p}).start()
            if i == 0:
                for other in hp:
                    kv_copy(part, z, h, part[3], {"heads": other}).start()

    q_sum = q_sum + jnp.dot(gained, wq[at, :], preferred_element_type=F32)
    queries = (q_sum * scale).astype(BF16).astype(F32)
    rotated = []
    for a in range(lh):
        qa = queries[:, a * KDIM : (a + 1) * KDIM]
        rotated.append((qa * qcos + pltpu.roll(qa, half, 1) * qsin).astype(BF16))

    for part in parts:
        kv_wait(part, part[0].at[z, pl.ds(0, H - 1)], part[3], z).wait_recv()
        for peer in zp:
            @pl.when(jnp.logical_not(direct(peer)))
            def _():
                for other in hp:
                    kv_copy(part, z, other, part[1], {"pos": peer}).start()

    load_wt.wait()
    for i in range(0, D, 128):
        wt[:, i : i + 128, :] = jnp.swapaxes(wraw[i : i + 128], 0, 1)
    score_parts, vts = [[] for _ in range(lh)], []
    for p in [z] + zp:
        if p is not z:
            kv_wait(parts[0], kbuf.at[p], ks, p).wait_recv()
        kt = jnp.concatenate([kbuf[p, i] for i in range(H)], axis=0).astype(F32)
        lo, hi = kt[:half], kt[half:]
        kt = jnp.concatenate(
            [lo * tabc[p] - hi * tabs[p], hi * tabc[p] + lo * tabs[p]], axis=0
        ).astype(BF16)
        for a in range(lh):
            score_parts[a].append(
                jnp.dot(rotated[a], kt, preferred_element_type=F32) * KDIM ** (-0.5)
            )
    for p in [z] + zp:
        if p is not z:
            kv_wait(parts[1], vbuf.at[p], vs, p).wait_recv()
        vts.append(jnp.concatenate([vbuf[p, i] for i in range(H)], axis=0))
    vt = jnp.concatenate(vts, axis=1)
    x = jnp.concatenate([xbuf[i, u] for i in range(H) for u in range(xunits)], axis=1)
    heads_out = []
    for a in range(lh):
        scores = jnp.concatenate(score_parts[a], axis=1)
        top = jnp.max(scores, axis=1, keepdims=True)
        weights = jnp.exp(scores - top)
        weight_sum = jnp.sum(weights, axis=1, keepdims=True)
        mixed = lax.dot_general(weights.astype(BF16), vt, NT, preferred_element_type=F32)
        heads_out.append(mixed / weight_sum)
    merged = jnp.concatenate(heads_out, axis=1).astype(BF16)

    load_wo.wait()
    uw = D // sum(GROUPS)
    edges = [sum(GROUPS[:c]) for c in range(NC + 1)]

    def part_copy(c, i, owner, slot):
        units = pl.ds(edges[c], GROUPS[c])
        return pltpu.make_async_remote_copy(
            psend.at[units], precv.at[owner, units], xs.at[0], xr.at[slot, c],
            device_id={"heads": hp[i]}, device_id_type=MESH,
        )

    kv_wait(parts[0], kbuf.at[z, pl.ds(0, H - 1)], xs.at[0], z).wait_send()
    for c in range(NC):
        lo, hi = edges[c] * uw, edges[c + 1] * uw
        part = jnp.dot(merged, wo[:, lo:hi], preferred_element_type=F32)
        rounded = part.astype(BF16)
        for u in range(GROUPS[c]):
            psend[edges[c] + u] = rounded[:, u * uw : (u + 1) * uw]
        for i in range(len(hp)):
            part_copy(c, i, h, H - 2 - i).start()
        own[:, lo:hi] = x[:, lo:hi].astype(F32) + part
    kv_wait(parts[1], vbuf.at[z, pl.ds(0, H - 1)], xs.at[1], z).wait_send()
    for part in parts:
        kv_wait(part, part[0].at[pl.ds(0, N - 1)], part[1], z).wait_send()
    load_tp.wait()
    hr = rows // 2
    swaps = []
    square = jnp.zeros((rows, 1), F32)
    blocks = cols // 128
    lane = lax.broadcasted_iota(jnp.int32, (1, 128), 1)
    stays = [
        tp_ref[b : b + 1, :] == (strand * H + h) * cols + b * 128 + lane for b in range(blocks)
    ]

    def cross(values, b, forward):
        swapped = jnp.where(lane % 2 == 0, pltpu.roll(values, 127, 1), pltpu.roll(values, 1, 1))
        return jnp.where(stays[b] | forward, values, swapped)

    for c in range(NC):
        a, e = edges[c] * uw, edges[c + 1] * uw
        summed = own[:, a:e]
        for i, peer in enumerate(hp):
            part_copy(c, i, peer, i).wait_recv()
            summed = summed + jnp.concatenate(
                [precv[peer, u].astype(F32) for u in range(edges[c], edges[c + 1])], axis=1
            )
        hidden = summed.astype(BF16).astype(F32)
        square = square + jnp.sum(hidden * hidden, axis=1, keepdims=True)
        gained = (hidden * spread(gains[1], a // 128, (e - a) // 128)).astype(BF16)
        last = c == NC - 1
        for s in (other_strand, strand):
            part = jnp.dot(gained, wt[s, a:e, :], preferred_element_type=F32)
            if c > 0:
                part = lg[s] + part
            if not last:
                lg[s] = part
                continue
            logits = part * lax.rsqrt(square / D + 1e-06)
            for r in range(2):
                part = logits[r * hr : (r + 1) * hr]
                track = (jnp.maximum(part, 0.0) + jnp.log1p(jnp.exp(-jnp.abs(part)))).astype(BF16)
                if s is strand:
                    for b in range(blocks):
                        at = slice(b * 128, (b + 1) * 128)
                        out_ref[r * hr : (r + 1) * hr, at] = 0.5 * cross(
                            track[:, at].astype(F32), b, fwd
                        )
                    continue
                snd[r] = track
                cp = pltpu.make_async_remote_copy(
                    snd.at[r], rcv.at[r], ss, sr.at[r],
                    device_id={"strand": other_strand}, device_id_type=MESH,
                )
                cp.start()
                swaps.append(cp)
    sent = precv.at[pl.ds(0, H - 1)]
    pltpu.make_async_remote_copy(
        sent, sent, xs.at[0], xr.at[0, 0], device_id={"heads": hp[0]}, device_id_type=MESH
    ).wait_send()
    for r in range(2):
        swaps[r].wait_recv()
        for b in range(blocks):
            at = slice(b * 128, (b + 1) * 128)
            rr = slice(r * hr, (r + 1) * hr)
            out_ref[rr, at] = out_ref[rr, at] + 0.5 * cross(
                rcv[r, :, at].astype(F32), b, jnp.logical_not(fwd)
            )
    pltpu.make_async_remote_copy(
        snd, rcv, ss, sr.at[0], device_id={"strand": other_strand}, device_id_type=MESH
    ).wait_send()


def store(src_ref, out_ref, sem):
    rows = src_ref.shape[0]
    step = rows // PARTS
    copies = [
        pltpu.make_async_copy(
            src_ref.at[pl.ds(i * step, step)], out_ref.at[pl.ds(i * step, step)], sem.at[i]
        )
        for i in range(PARTS)
    ]
    for cp in copies:
        cp.start()
    for cp in copies:
        cp.wait()


def body(
    base_codes, embed_table, attn_gain, w_query, w_key, w_value, w_out, head_gain, w_tracks, track_pairs
):
    H = lax.axis_size("heads")
    N = lax.axis_size("pos")
    rows = base_codes.shape[0] // BIN
    dl = embed_table.shape[1]
    D = dl * H
    cols = w_tracks.shape[2]
    kvl = w_key.shape[1] + w_value.shape[1]
    NC, NX = len(GROUPS), 3
    vm = pl.BlockSpec(memory_space=pltpu.VMEM)
    hbm = pl.BlockSpec(memory_space=pl.ANY)
    dma = pltpu.SemaphoreType.DMA
    hm = max(H - 1, 1)
    tracks = pl.pallas_call(
        functools.partial(kernel, H, N, NC, NX),
        out_shape=pltpu.VMEM((rows, cols), F32),
        in_specs=[hbm] * 10,
        out_specs=vm,
        scratch_shapes=[
            pltpu.VMEM((cols // 128, 128), jnp.int32),
            pltpu.VMEM((rows, BIN), jnp.int32),
            pltpu.VMEM((2, D // 128, 128), F32),
            pltpu.VMEM(embed_table.shape, BF16),
            pltpu.VMEM(w_query.shape, BF16),
            pltpu.VMEM((kvl, D), BF16),
            pltpu.VMEM(w_out.shape, BF16),
            pltpu.VMEM(w_tracks.shape, BF16),
            pltpu.VMEM((2, D, cols), BF16),
            pltpu.VMEM((H, dl // 128, rows, 128), BF16),
            pltpu.VMEM((N, H, w_key.shape[1], rows), BF16),
            pltpu.VMEM((N, H, w_value.shape[1], rows), BF16),
            pltpu.VMEM((N, KDIM // 2, rows), F32),
            pltpu.VMEM((N, KDIM // 2, rows), F32),
            pltpu.VMEM((rows, D), F32),
            pltpu.VMEM((sum(GROUPS), rows, D // sum(GROUPS)), BF16),
            pltpu.VMEM((H, sum(GROUPS), rows, D // sum(GROUPS)), BF16),
            pltpu.VMEM((2, rows, cols), F32),
            pltpu.VMEM((2, rows // 2, cols), BF16),
            pltpu.VMEM((2, rows // 2, cols), BF16),
            dma((3 + NX,)),
            dma((2,)),
            dma((hm, NC)),
            dma,
            dma,
            dma((N,)),
            dma((N,)),
            dma,
            dma((2,)),
            pltpu.SemaphoreType.REGULAR,
            pltpu.SemaphoreType.REGULAR,
        ],
        compiler_params=pltpu.CompilerParams(
            collective_id=0, has_side_effects=True, vmem_limit_bytes=60 * 1024 * 1024
        ),
    )(
        base_codes.reshape(rows, BIN),
        embed_table,
        attn_gain.reshape(D // 128, 128),
        w_query,
        w_key.T,
        w_value.T,
        w_out,
        head_gain.reshape(D // 128, 128),
        w_tracks,
        track_pairs.reshape(cols // 128, 128),
    )
    return tracks


def solution(mesh):
    placed = (
        P(("groups", "pos")),
        P(None, "heads"),
        P(),
        P(None, "heads"),
        P(None, "heads"),
        P(None, "heads"),
        P("heads", None),
        P(),
        P(None, None, "heads"),
        P(("strand", "heads")),
    )
    return jax.shard_map(
        body,
        mesh=mesh,
        in_specs=placed,
        out_specs=P(("groups", "pos"), ("strand", "heads")),
        check_vma=False,
    )
```

```python
import functools
import math

import jax
import jax.numpy as jnp
from jax import lax
from jax.experimental import pallas as pl
from jax.experimental.pallas import tpu as pltpu
from jax.sharding import PartitionSpec as P

KDIM = 128
VDIM = 192
BIN = 128
F32 = jnp.float32
BF16 = jnp.bfloat16
MESH = pl.DeviceIdType.MESH
NT = (((1,), (1,)), ((), ()))
FIRST = 1
GROUPS = (2, 3, 3, 2, 2)


def spread(table, first, count):
    return jnp.concatenate([table[first + i : first + i + 1, :] for i in range(count)], axis=1)


def partner(z, step, N):
    if N & (N - 1):
        return lax.rem(z + step, N)
    bit = 1
    while bit < N:
        if step & bit:
            z = z + bit - 2 * bit * ((z // bit) % 2)
        bit *= 2
    return z


def kernel(
    H, N, NC, NX,
    codes_hbm, et_hbm, g1_hbm, wq_hbm, wk_hbm, wv_hbm, wo_hbm, g2_hbm, wt_hbm, tp_hbm,
    out_ref,
    tp_ref, codes_ref, gains, et, wq, wkv, wo, wraw, wt, xbuf, kbuf, vbuf, tabc, tabs, own, psend, precv, lg, snd, rcv,
    ls, xs, xr, ks, vs, kr, vr, ss, sr, ready, turn,
):
    h = lax.axis_index("heads")
    z = lax.axis_index("pos")
    strand = lax.axis_index("strand")
    rows = codes_hbm.shape[0]
    dl = et.shape[1]
    D = dl * H
    kl = wk_hbm.shape[0]
    kvl = wkv.shape[0]
    lh = wq.shape[1] // KDIM
    cols = wt.shape[2]
    total = rows * N

    hp = [lax.rem(h + i, H) for i in range(1, H)]
    zp = [partner(z, i, N) for i in range(1, N)]
    other_strand = 1 - strand

    def direct(p):
        return (4 * p < N) | (2 * (z - p) >= N) | ((strand == FIRST) & (z - p == 1))

    barrier = pltpu.get_barrier_semaphore()

    def greet(sem, up):
        for peer in zp:
            @pl.when(peer > z if up else peer < z)
            def _():
                for other in [h] + hp:
                    pl.semaphore_signal(
                        sem, inc=1, device_id={"pos": peer, "heads": other}, device_id_type=MESH
                    )

    greet(barrier, True)
    for peer in hp:
        pl.semaphore_signal(barrier, inc=1, device_id={"heads": peer}, device_id_type=MESH)
    pl.semaphore_signal(barrier, inc=1, device_id={"strand": other_strand}, device_id_type=MESH)

    xunits = dl // 128
    lead = max(1, xunits // 3)
    after = max(1, xunits // 6)
    xsizes = (lead, after, xunits - lead - after)
    xat = [sum(xsizes[:c]) for c in range(NX + 1)]
    load_codes = pltpu.make_async_copy(codes_hbm, codes_ref, ls.at[0])
    load_wq = pltpu.make_async_copy(wq_hbm, wq, ls.at[0])
    load_et = [
        pltpu.make_async_copy(
            et_hbm.at[:, pl.ds(xat[c] * 128, xsizes[c] * 128)],
            et.at[:, pl.ds(xat[c] * 128, xsizes[c] * 128)],
            ls.at[1 + c],
        )
        for c in range(NX)
    ]
    load_tp = pltpu.make_async_copy(tp_hbm, tp_ref, ls.at[1])
    load_wt = pltpu.make_async_copy(wt_hbm, wraw, ls.at[2])
    load_wo = pltpu.make_async_copy(wo_hbm, wo, ls.at[3])
    load_codes.start()
    for cp in load_et:
        cp.start()
    pltpu.make_async_copy(g1_hbm, gains.at[0], ls.at[1 + NX]).start()
    pltpu.make_async_copy(g2_hbm, gains.at[1], ls.at[1 + NX]).start()

    fwd = strand == 0
    width = 4 * BIN
    src_row = lax.broadcasted_iota(jnp.int32, (BIN, width), 0)
    place = lax.broadcasted_iota(jnp.int32, (BIN, width), 1) // 4
    want = jnp.where(fwd, place, BIN - 1 - place)
    expand = (src_row == want).astype(F32).astype(BF16)
    load_codes.wait()
    repeated = jnp.dot(codes_ref[...].astype(F32).astype(BF16), expand, preferred_element_type=F32)
    letter = lax.broadcasted_iota(jnp.int32, (rows, width), 1) % 4
    letter = jnp.where(fwd, letter, 3 - letter).astype(F32)
    onehot = (repeated == letter).astype(F32).astype(BF16)

    pltpu.make_async_copy(wk_hbm, wkv.at[pl.ds(0, kl), :], ls.at[2 + NX]).start()
    pltpu.make_async_copy(wv_hbm, wkv.at[pl.ds(kl, kvl - kl), :], ls.at[2 + NX]).start()
    load_wq.start()
    gate = max(NX - 2, 0)

    def x_copy(i, c):
        ref = xbuf.at[h, pl.ds(xat[c], xsizes[c])]
        return pltpu.make_async_remote_copy(
            ref, ref, xs.at[int(c > gate)], xr.at[H - 2 - i, int(c > gate)],
            device_id={"heads": hp[i]}, device_id_type=MESH,
        )

    def x_wait(part, i, count, first):
        units = pl.ds(0, xat[gate + 1]) if part == 0 else pl.ds(xat[gate + 1], xat[NX] - xat[gate + 1])
        ref = xbuf.at[pl.ds(first, count), units]
        return pltpu.make_async_remote_copy(
            ref, ref, xs.at[part], xr.at[i, part], device_id={"heads": hp[i]}, device_id_type=MESH
        )

    for c in range(NX):
        load_et[c].wait()
        part = jnp.dot(
            onehot, et[:, xat[c] * 128 : xat[c + 1] * 128], preferred_element_type=F32
        ).astype(BF16)
        for u in range(xsizes[c]):
            xbuf[h, xat[c] + u] = part[:, u * 128 : (u + 1) * 128]
        if c == 0:
            pl.semaphore_wait(barrier, len(hp) + 1 + z * H)
            greet(ready, False)

        @pl.when(strand == FIRST)
        def _():
            for i in range(len(hp)):
                x_copy(i, c).start()
    load_wt.start()
    load_wo.start()
    load_tp.start()

    half = KDIM // 2
    step = -math.log(10000.0) / half
    lane_pos = lax.broadcasted_iota(jnp.int32, (half, rows), 1)
    kinv = jnp.exp(lax.broadcasted_iota(jnp.int32, (half, rows), 0).astype(F32) * step)
    for p in range(N):
        pos = lane_pos + p * rows
        pos = jnp.where(fwd, pos, total - 1 - pos).astype(F32)
        tabc[p] = jnp.cos(pos * kinv)
        tabs[p] = jnp.sin(pos * kinv)
    qpos = lax.broadcasted_iota(jnp.int32, (rows, KDIM), 0) + z * rows
    qpos = jnp.where(fwd, qpos, total - 1 - qpos).astype(F32)
    qlane = lax.broadcasted_iota(jnp.int32, (rows, KDIM), 1)
    qang = qpos * jnp.exp((qlane % half).astype(F32) * step)
    qcos = jnp.cos(qang)
    qsin = jnp.where(qlane < half, -1.0, 1.0) * jnp.sin(qang)


    @pl.when(strand == FIRST)
    def _():
        x_wait(0, 0, H - 1, 0).wait_send()
        pl.semaphore_signal(turn, inc=1, device_id={"strand": other_strand}, device_id_type=MESH)

    @pl.when(strand != FIRST)
    def _():
        pl.semaphore_wait(turn, 1)
        for c in range(NX):
            for i in range(len(hp)):
                x_copy(i, c).start()


    pltpu.make_async_copy(gains, gains, ls.at[1 + NX]).wait()
    pltpu.make_async_copy(wkv, wkv, ls.at[2 + NX]).wait()
    load_wq.wait()
    kv_sum = jnp.zeros((kvl, rows), F32)
    q_sum = jnp.zeros((rows, lh * KDIM), F32)
    total_square = jnp.zeros((rows, 1), F32)
    for k, peer in enumerate([h] + hp):
        for c in range(NX):
            if k == 1 and c == 0:
                @pl.when(strand != FIRST)
                def _():
                    x_wait(0, 0, H - 1, 0).wait_send()

                x_wait(1, 0, H - 1, 0).wait_send()
            if k > 0 and c in (0, gate + 1):
                x_wait(int(c > gate), k - 1, 1, peer).wait_recv()
            piece = jnp.concatenate(
                [xbuf[peer, u].astype(F32) for u in range(xat[c], xat[c + 1])], axis=1
            )
            total_square = total_square + jnp.sum(piece * piece, axis=1, keepdims=True)
            first = peer * dl + xat[c] * 128
            gain = jnp.concatenate(
                [gains[0, pl.ds(first // 128 + j, 1), :] for j in range(xsizes[c])], axis=1
            )
            gained = (piece * gain).astype(BF16)
            at = pl.ds(pl.multiple_of(first, 128), xsizes[c] * 128)
            kv_sum = kv_sum + lax.dot_general(wkv[:, at], gained, NT, preferred_element_type=F32)
            if peer is hp[-1] and c == NX - 1:
                break
            q_sum = q_sum + jnp.dot(gained, wq[at, :], preferred_element_type=F32)
    scale = lax.rsqrt(total_square / D + 1e-06)
    scale_row = jnp.transpose(jnp.broadcast_to(scale, (rows, 128)))[:1, :]
    kv_own = (kv_sum * scale_row).astype(BF16)
    kbuf[z, h] = kv_own[:kl]
    vbuf[z, h] = kv_own[kl:]
    parts = ((kbuf, ks, kr, xs.at[0]), (vbuf, vs, vr, xs.at[1]))

    def kv_copy(part, p, hh, send, target):
        buf, _, recv, _ = part
        return pltpu.make_async_remote_copy(
            buf.at[p, hh], buf.at[p, hh], send, recv.at[p], device_id=target, device_id_type=MESH
        )

    def kv_wait(part, ref, send, p):
        return pltpu.make_async_remote_copy(
            ref, ref, send, part[2].at[p], device_id={"heads": hp[0]}, device_id_type=MESH
        )

    @pl.when(z < N - 1)
    def _():
        pl.semaphore_wait(ready, (N - 1 - z) * H)

    for i in range(N - 1):
        p = jnp.where(z <= i, i + 1, i)

        @pl.when(direct(p))
        def _():
            for part in parts:
                for other in hp:
                    kv_copy(part, z, h, part[1], {"pos": p, "heads": other}).start()

        for part in parts:
            kv_copy(part, z, h, part[1], {"pos": p}).start()
            if i == 0:
                for other in hp:
                    kv_copy(part, z, h, part[3], {"heads": other}).start()

    q_sum = q_sum + jnp.dot(gained, wq[at, :], preferred_element_type=F32)
    queries = (q_sum * scale).astype(BF16).astype(F32)
    rotated = []
    for a in range(lh):
        qa = queries[:, a * KDIM : (a + 1) * KDIM]
        rotated.append((qa * qcos + pltpu.roll(qa, half, 1) * qsin).astype(BF16))

    for part in parts:
        kv_wait(part, part[0].at[z, pl.ds(0, H - 1)], part[3], z).wait_recv()
        for i in range(N - 1):
            peer = jnp.where(z <= i, i + 1, i)

            @pl.when(jnp.logical_not(direct(peer)))
            def _():
                for other in hp:
                    kv_copy(part, z, other, part[1], {"pos": peer}).start()

    load_wt.wait()
    for i in range(0, D, 128):
        wt[:, i : i + 128, :] = jnp.swapaxes(wraw[i : i + 128], 0, 1)
    score_parts, vts = [[] for _ in range(lh)], []
    for p in [z] + zp:
        if p is not z:
            kv_wait(parts[0], kbuf.at[p], ks, p).wait_recv()
        kt = jnp.concatenate([kbuf[p, i] for i in range(H)], axis=0).astype(F32)
        lo, hi = kt[:half], kt[half:]
        kt = jnp.concatenate(
            [lo * tabc[p] - hi * tabs[p], hi * tabc[p] + lo * tabs[p]], axis=0
        ).astype(BF16)
        for a in range(lh):
            score_parts[a].append(
                jnp.dot(rotated[a], kt, preferred_element_type=F32) * KDIM ** (-0.5)
            )
    for p in [z] + zp:
        if p is not z:
            kv_wait(parts[1], vbuf.at[p], vs, p).wait_recv()
        vts.append(jnp.concatenate([vbuf[p, i] for i in range(H)], axis=0))
    vt = jnp.concatenate(vts, axis=1)
    x = jnp.concatenate([xbuf[i, u] for i in range(H) for u in range(xunits)], axis=1)
    heads_out = []
    for a in range(lh):
        scores = jnp.concatenate(score_parts[a], axis=1)
        top = jnp.max(scores, axis=1, keepdims=True)
        weights = jnp.exp(scores - top)
        weight_sum = jnp.sum(weights, axis=1, keepdims=True)
        mixed = lax.dot_general(weights.astype(BF16), vt, NT, preferred_element_type=F32)
        heads_out.append(mixed / weight_sum)
    merged = jnp.concatenate(heads_out, axis=1).astype(BF16)

    load_wo.wait()
    uw = D // sum(GROUPS)
    edges = [sum(GROUPS[:c]) for c in range(NC + 1)]

    def part_copy(c, i, owner, slot):
        units = pl.ds(edges[c], GROUPS[c])
        return pltpu.make_async_remote_copy(
            psend.at[units], precv.at[owner, units], xs.at[0], xr.at[slot, c],
            device_id={"heads": hp[i]}, device_id_type=MESH,
        )

    kv_wait(parts[0], kbuf.at[z, pl.ds(0, H - 1)], xs.at[0], z).wait_send()
    for c in range(NC):
        lo, hi = edges[c] * uw, edges[c + 1] * uw
        part = jnp.dot(merged, wo[:, lo:hi], preferred_element_type=F32)
        rounded = part.astype(BF16)
        for u in range(GROUPS[c]):
            psend[edges[c] + u] = rounded[:, u * uw : (u + 1) * uw]
        for i in range(len(hp)):
            part_copy(c, i, h, H - 2 - i).start()
        own[:, lo:hi] = x[:, lo:hi].astype(F32) + part
    kv_wait(parts[1], vbuf.at[z, pl.ds(0, H - 1)], xs.at[1], z).wait_send()
    for part in parts:
        kv_wait(part, part[0].at[pl.ds(0, N - 1)], part[1], z).wait_send()
    load_tp.wait()
    hr = rows // 2
    swaps = []
    square = jnp.zeros((rows, 1), F32)
    blocks = cols // 128
    lane = lax.broadcasted_iota(jnp.int32, (1, 128), 1)
    stays = [
        tp_ref[b : b + 1, :] == (strand * H + h) * cols + b * 128 + lane for b in range(blocks)
    ]

    def cross(values, b, forward):
        swapped = jnp.where(lane % 2 == 0, pltpu.roll(values, 127, 1), pltpu.roll(values, 1, 1))
        return jnp.where(stays[b] | forward, values, swapped)

    for c in range(NC):
        a, e = edges[c] * uw, edges[c + 1] * uw
        summed = own[:, a:e]
        for i, peer in enumerate(hp):
            part_copy(c, i, peer, i).wait_recv()
            summed = summed + jnp.concatenate(
                [precv[peer, u].astype(F32) for u in range(edges[c], edges[c + 1])], axis=1
            )
        hidden = summed.astype(BF16).astype(F32)
        square = square + jnp.sum(hidden * hidden, axis=1, keepdims=True)
        gained = (hidden * spread(gains[1], a // 128, (e - a) // 128)).astype(BF16)
        last = c == NC - 1
        for s in (other_strand, strand):
            part = jnp.dot(gained, wt[s, a:e, :], preferred_element_type=F32)
            if c > 0:
                part = lg[s] + part
            if not last:
                lg[s] = part
                continue
            logits = part * lax.rsqrt(square / D + 1e-06)
            for r in range(2):
                part = logits[r * hr : (r + 1) * hr]
                track = (jnp.maximum(part, 0.0) + jnp.log1p(jnp.exp(-jnp.abs(part)))).astype(BF16)
                if s is strand:
                    for b in range(blocks):
                        at = slice(b * 128, (b + 1) * 128)
                        out_ref[r * hr : (r + 1) * hr, at] = 0.5 * cross(
                            track[:, at].astype(F32), b, fwd
                        )
                    continue
                snd[r] = track
                cp = pltpu.make_async_remote_copy(
                    snd.at[r], rcv.at[r], ss, sr.at[r],
                    device_id={"strand": other_strand}, device_id_type=MESH,
                )
                cp.start()
                swaps.append(cp)
    sent = precv.at[pl.ds(0, H - 1)]
    pltpu.make_async_remote_copy(
        sent, sent, xs.at[0], xr.at[0, 0], device_id={"heads": hp[0]}, device_id_type=MESH
    ).wait_send()
    for r in range(2):
        swaps[r].wait_recv()
        for b in range(blocks):
            at = slice(b * 128, (b + 1) * 128)
            rr = slice(r * hr, (r + 1) * hr)
            out_ref[rr, at] = out_ref[rr, at] + 0.5 * cross(
                rcv[r, :, at].astype(F32), b, jnp.logical_not(fwd)
            )
    pltpu.make_async_remote_copy(
        snd, rcv, ss, sr.at[0], device_id={"strand": other_strand}, device_id_type=MESH
    ).wait_send()


def body(
    base_codes, embed_table, attn_gain, w_query, w_key, w_value, w_out, head_gain, w_tracks, track_pairs
):
    H = lax.axis_size("heads")
    N = lax.axis_size("pos")
    rows = base_codes.shape[0] // BIN
    dl = embed_table.shape[1]
    D = dl * H
    cols = w_tracks.shape[2]
    kvl = w_key.shape[1] + w_value.shape[1]
    NC, NX = len(GROUPS), 3
    vm = pl.BlockSpec(memory_space=pltpu.VMEM)
    hbm = pl.BlockSpec(memory_space=pl.ANY)
    dma = pltpu.SemaphoreType.DMA
    hm = max(H - 1, 1)
    tracks = pl.pallas_call(
        functools.partial(kernel, H, N, NC, NX),
        out_shape=pltpu.VMEM((rows, cols), F32),
        in_specs=[hbm] * 10,
        out_specs=vm,
        scratch_shapes=[
            pltpu.VMEM((cols // 128, 128), jnp.int32),
            pltpu.VMEM((rows, BIN), jnp.int32),
            pltpu.VMEM((2, D // 128, 128), F32),
            pltpu.VMEM(embed_table.shape, BF16),
            pltpu.VMEM(w_query.shape, BF16),
            pltpu.VMEM((kvl, D), BF16),
            pltpu.VMEM(w_out.shape, BF16),
            pltpu.VMEM(w_tracks.shape, BF16),
            pltpu.VMEM((2, D, cols), BF16),
            pltpu.VMEM((H, dl // 128, rows, 128), BF16),
            pltpu.VMEM((N, H, w_key.shape[1], rows), BF16),
            pltpu.VMEM((N, H, w_value.shape[1], rows), BF16),
            pltpu.VMEM((N, KDIM // 2, rows), F32),
            pltpu.VMEM((N, KDIM // 2, rows), F32),
            pltpu.VMEM((rows, D), F32),
            pltpu.VMEM((sum(GROUPS), rows, D // sum(GROUPS)), BF16),
            pltpu.VMEM((H, sum(GROUPS), rows, D // sum(GROUPS)), BF16),
            pltpu.VMEM((2, rows, cols), F32),
            pltpu.VMEM((2, rows // 2, cols), BF16),
            pltpu.VMEM((2, rows // 2, cols), BF16),
            dma((3 + NX,)),
            dma((2,)),
            dma((hm, NC)),
            dma,
            dma,
            dma((N,)),
            dma((N,)),
            dma,
            dma((2,)),
            pltpu.SemaphoreType.REGULAR,
            pltpu.SemaphoreType.REGULAR,
        ],
        compiler_params=pltpu.CompilerParams(
            collective_id=0, has_side_effects=True, vmem_limit_bytes=60 * 1024 * 1024
        ),
    )(
        base_codes.reshape(rows, BIN),
        embed_table,
        attn_gain.reshape(D // 128, 128),
        w_query,
        w_key.T,
        w_value.T,
        w_out,
        head_gain.reshape(D // 128, 128),
        w_tracks,
        track_pairs.reshape(cols // 128, 128),
    )
    return tracks


def solution(mesh):
    placed = (
        P(("groups", "pos")),
        P(None, "heads"),
        P(),
        P(None, "heads"),
        P(None, "heads"),
        P(None, "heads"),
        P("heads", None),
        P(),
        P(None, None, "heads"),
        P(("strand", "heads")),
    )
    return jax.shard_map(
        body,
        mesh=mesh,
        in_specs=placed,
        out_specs=P(("groups", "pos"), ("strand", "heads")),
        check_vma=False,
    )
```

```python
import functools
import math

import jax
import jax.numpy as jnp
from jax import lax
from jax.experimental import pallas as pl
from jax.experimental.pallas import tpu as pltpu
from jax.sharding import PartitionSpec as P

KDIM = 128
VDIM = 192
BIN = 128
F32 = jnp.float32
BF16 = jnp.bfloat16
MESH = pl.DeviceIdType.MESH
NT = (((1,), (1,)), ((), ()))
FIRST = 1
GROUPS = (2, 3, 3, 2, 2)


def spread(table, first, count):
    return jnp.concatenate([table[first + i : first + i + 1, :] for i in range(count)], axis=1)


def partner(z, step, N):
    if N & (N - 1):
        return lax.rem(z + step, N)
    bit = 1
    while bit < N:
        if step & bit:
            z = z + bit - 2 * bit * ((z // bit) % 2)
        bit *= 2
    return z


def kernel(
    H, N, NC, NX,
    codes_hbm, et_hbm, g1_hbm, wq_hbm, wk_hbm, wv_hbm, wo_hbm, g2_hbm, wt_hbm, tp_hbm,
    out_ref,
    tp_ref, codes_ref, gains, et, wq, wkv, wo, wraw, wt, xbuf, kbuf, vbuf, tabc, tabs, own, psend, precv, lg, snd, rcv,
    ls, xs, xr, ks, vs, kr, vr, ss, sr, ready, turn,
):
    h = lax.axis_index("heads")
    z = lax.axis_index("pos")
    strand = lax.axis_index("strand")
    rows = codes_hbm.shape[0]
    dl = et.shape[1]
    D = dl * H
    kl = wk_hbm.shape[0]
    kvl = wkv.shape[0]
    lh = wq.shape[1] // KDIM
    cols = wt.shape[2]
    total = rows * N

    hp = [lax.rem(h + i, H) for i in range(1, H)]
    zp = [partner(z, i, N) for i in range(1, N)]
    other_strand = 1 - strand

    def direct(p):
        return (4 * p < N) | (2 * (z - p) >= N) | ((strand == FIRST) & (z - p == 1))

    barrier = pltpu.get_barrier_semaphore()

    def greet(sem, up):
        for peer in zp:
            @pl.when(peer > z if up else peer < z)
            def _():
                for other in [h] + hp:
                    pl.semaphore_signal(
                        sem, inc=1, device_id={"pos": peer, "heads": other}, device_id_type=MESH
                    )

    greet(barrier, True)
    for peer in hp:
        pl.semaphore_signal(barrier, inc=1, device_id={"heads": peer}, device_id_type=MESH)
    pl.semaphore_signal(barrier, inc=1, device_id={"strand": other_strand}, device_id_type=MESH)

    xunits = dl // 128
    lead = max(1, xunits // 3)
    after = max(1, xunits // 6)
    rest = xunits - lead - after
    xsizes = (lead, after, rest - 1, 1) if NX > 3 else (lead, after, rest)
    xat = [sum(xsizes[:c]) for c in range(NX + 1)]
    load_codes = pltpu.make_async_copy(codes_hbm, codes_ref, ls.at[0])
    load_wq = pltpu.make_async_copy(wq_hbm, wq, ls.at[0])
    load_et = [
        pltpu.make_async_copy(
            et_hbm.at[:, pl.ds(xat[c] * 128, xsizes[c] * 128)],
            et.at[:, pl.ds(xat[c] * 128, xsizes[c] * 128)],
            ls.at[1 + c],
        )
        for c in range(NX)
    ]
    load_tp = pltpu.make_async_copy(tp_hbm, tp_ref, ls.at[1])
    load_wt = pltpu.make_async_copy(wt_hbm, wraw, ls.at[2])
    load_wo = pltpu.make_async_copy(wo_hbm, wo, ls.at[3])
    load_codes.start()
    for cp in load_et:
        cp.start()
    pltpu.make_async_copy(g1_hbm, gains.at[0], ls.at[1 + NX]).start()
    pltpu.make_async_copy(g2_hbm, gains.at[1], ls.at[1 + NX]).start()

    fwd = strand == 0
    width = 4 * BIN
    src_row = lax.broadcasted_iota(jnp.int32, (BIN, width), 0)
    place = lax.broadcasted_iota(jnp.int32, (BIN, width), 1) // 4
    want = jnp.where(fwd, place, BIN - 1 - place)
    expand = (src_row == want).astype(F32).astype(BF16)
    load_codes.wait()
    repeated = jnp.dot(codes_ref[...].astype(F32).astype(BF16), expand, preferred_element_type=F32)
    letter = lax.broadcasted_iota(jnp.int32, (rows, width), 1) % 4
    letter = jnp.where(fwd, letter, 3 - letter).astype(F32)
    onehot = (repeated == letter).astype(F32).astype(BF16)

    pltpu.make_async_copy(wk_hbm, wkv.at[pl.ds(0, kl), :], ls.at[2 + NX]).start()
    pltpu.make_async_copy(wv_hbm, wkv.at[pl.ds(kl, kvl - kl), :], ls.at[2 + NX]).start()
    load_wq.start()
    gate = 1

    def x_copy(i, c):
        ref = xbuf.at[h, pl.ds(xat[c], xsizes[c])]
        return pltpu.make_async_remote_copy(
            ref, ref, xs.at[int(c > gate)], xr.at[H - 2 - i, max(c - gate, 0)],
            device_id={"heads": hp[i]}, device_id_type=MESH,
        )

    def x_wait(part, i, count, first, start, end):
        ref = xbuf.at[pl.ds(first, count), pl.ds(xat[start], xat[end] - xat[start])]
        return pltpu.make_async_remote_copy(
            ref, ref, xs.at[min(part, 1)], xr.at[i, part], device_id={"heads": hp[i]}, device_id_type=MESH
        )

    for c in range(NX):
        load_et[c].wait()
        part = jnp.dot(
            onehot, et[:, xat[c] * 128 : xat[c + 1] * 128], preferred_element_type=F32
        ).astype(BF16)
        for u in range(xsizes[c]):
            xbuf[h, xat[c] + u] = part[:, u * 128 : (u + 1) * 128]
        if c == 0:
            pl.semaphore_wait(barrier, len(hp) + 1 + z * H)
            greet(ready, False)

        @pl.when(strand == FIRST)
        def _():
            for i in range(len(hp)):
                x_copy(i, c).start()
    load_wt.start()
    load_wo.start()
    load_tp.start()

    half = KDIM // 2
    step = -math.log(10000.0) / half
    lane_pos = lax.broadcasted_iota(jnp.int32, (half, rows), 1)
    kinv = jnp.exp(lax.broadcasted_iota(jnp.int32, (half, rows), 0).astype(F32) * step)
    for p in range(N):
        pos = lane_pos + p * rows
        pos = jnp.where(fwd, pos, total - 1 - pos).astype(F32)
        tabc[p] = jnp.cos(pos * kinv)
        tabs[p] = jnp.sin(pos * kinv)
    qpos = lax.broadcasted_iota(jnp.int32, (rows, KDIM), 0) + z * rows
    qpos = jnp.where(fwd, qpos, total - 1 - qpos).astype(F32)
    qlane = lax.broadcasted_iota(jnp.int32, (rows, KDIM), 1)
    qang = qpos * jnp.exp((qlane % half).astype(F32) * step)
    qcos = jnp.cos(qang)
    qsin = jnp.where(qlane < half, -1.0, 1.0) * jnp.sin(qang)


    @pl.when(strand == FIRST)
    def _():
        x_wait(0, 0, H - 1, 0, 0, gate + 1).wait_send()
        pl.semaphore_signal(turn, inc=1, device_id={"strand": other_strand}, device_id_type=MESH)

    @pl.when(strand != FIRST)
    def _():
        pl.semaphore_wait(turn, 1)
        for c in range(NX):
            for i in range(len(hp)):
                x_copy(i, c).start()


    pltpu.make_async_copy(gains, gains, ls.at[1 + NX]).wait()
    pltpu.make_async_copy(wkv, wkv, ls.at[2 + NX]).wait()
    load_wq.wait()
    kv_sum = jnp.zeros((kvl, rows), F32)
    q_sum = jnp.zeros((rows, lh * KDIM), F32)
    total_square = jnp.zeros((rows, 1), F32)
    for k, peer in enumerate([h] + hp):
        for c in range(NX):
            if k == 1 and c == 0:
                @pl.when(strand != FIRST)
                def _():
                    x_wait(0, 0, H - 1, 0, 0, gate + 1).wait_send()

                x_wait(1, 0, H - 1, 0, gate + 1, NX).wait_send()
            if k > 0 and c == 0:
                x_wait(0, k - 1, 1, peer, 0, gate + 1).wait_recv()
            if k > 0 and c > gate:
                x_wait(c - gate, k - 1, 1, peer, c, c + 1).wait_recv()
            piece = jnp.concatenate(
                [xbuf[peer, u].astype(F32) for u in range(xat[c], xat[c + 1])], axis=1
            )
            total_square = total_square + jnp.sum(piece * piece, axis=1, keepdims=True)
            first = peer * dl + xat[c] * 128
            gain = jnp.concatenate(
                [gains[0, pl.ds(first // 128 + j, 1), :] for j in range(xsizes[c])], axis=1
            )
            gained = (piece * gain).astype(BF16)
            at = pl.ds(pl.multiple_of(first, 128), xsizes[c] * 128)
            kv_sum = kv_sum + lax.dot_general(wkv[:, at], gained, NT, preferred_element_type=F32)
            if peer is hp[-1] and c == NX - 1:
                break
            q_sum = q_sum + jnp.dot(gained, wq[at, :], preferred_element_type=F32)
    scale = lax.rsqrt(total_square / D + 1e-06)
    scale_row = jnp.transpose(jnp.broadcast_to(scale, (rows, 128)))[:1, :]
    kv_own = (kv_sum * scale_row).astype(BF16)
    kbuf[z, h] = kv_own[:kl]
    vbuf[z, h] = kv_own[kl:]
    parts = ((kbuf, ks, kr, xs.at[0]), (vbuf, vs, vr, xs.at[1]))

    def kv_copy(part, p, hh, send, target):
        buf, _, recv, _ = part
        return pltpu.make_async_remote_copy(
            buf.at[p, hh], buf.at[p, hh], send, recv.at[p], device_id=target, device_id_type=MESH
        )

    def kv_wait(part, ref, send, p):
        return pltpu.make_async_remote_copy(
            ref, ref, send, part[2].at[p], device_id={"heads": hp[0]}, device_id_type=MESH
        )

    @pl.when(z < N - 1)
    def _():
        pl.semaphore_wait(ready, (N - 1 - z) * H)

    for i in range(N - 1):
        p = jnp.where(z <= i, i + 1, i)

        @pl.when(direct(p))
        def _():
            for part in parts:
                for other in hp:
                    kv_copy(part, z, h, part[1], {"pos": p, "heads": other}).start()

        for part in parts:
            kv_copy(part, z, h, part[1], {"pos": p}).start()
            if i == 0:
                for other in hp:
                    kv_copy(part, z, h, part[3], {"heads": other}).start()

    q_sum = q_sum + jnp.dot(gained, wq[at, :], preferred_element_type=F32)
    queries = (q_sum * scale).astype(BF16).astype(F32)
    rotated = []
    for a in range(lh):
        qa = queries[:, a * KDIM : (a + 1) * KDIM]
        rotated.append((qa * qcos + pltpu.roll(qa, half, 1) * qsin).astype(BF16))

    for part in parts:
        kv_wait(part, part[0].at[z, pl.ds(0, H - 1)], part[3], z).wait_recv()
        for i in range(N - 1):
            peer = jnp.where(z <= i, i + 1, i)

            @pl.when(jnp.logical_not(direct(peer)))
            def _():
                for other in hp:
                    kv_copy(part, z, other, part[1], {"pos": peer}).start()

    load_wt.wait()
    for i in range(0, D, 128):
        wt[:, i : i + 128, :] = jnp.swapaxes(wraw[i : i + 128], 0, 1)
    score_parts, vts = [[] for _ in range(lh)], []
    for p in [z] + zp:
        if p is not z:
            kv_wait(parts[0], kbuf.at[p], ks, p).wait_recv()
        kt = jnp.concatenate([kbuf[p, i] for i in range(H)], axis=0).astype(F32)
        lo, hi = kt[:half], kt[half:]
        kt = jnp.concatenate(
            [lo * tabc[p] - hi * tabs[p], hi * tabc[p] + lo * tabs[p]], axis=0
        ).astype(BF16)
        for a in range(lh):
            score_parts[a].append(
                jnp.dot(rotated[a], kt, preferred_element_type=F32) * KDIM ** (-0.5)
            )
    for p in [z] + zp:
        if p is not z:
            kv_wait(parts[1], vbuf.at[p], vs, p).wait_recv()
        vts.append(jnp.concatenate([vbuf[p, i] for i in range(H)], axis=0))
    vt = jnp.concatenate(vts, axis=1)
    x = jnp.concatenate([xbuf[i, u] for i in range(H) for u in range(xunits)], axis=1)
    heads_out = []
    for a in range(lh):
        scores = jnp.concatenate(score_parts[a], axis=1)
        top = jnp.max(scores, axis=1, keepdims=True)
        weights = jnp.exp(scores - top)
        weight_sum = jnp.sum(weights, axis=1, keepdims=True)
        mixed = lax.dot_general(weights.astype(BF16), vt, NT, preferred_element_type=F32)
        heads_out.append(mixed / weight_sum)
    merged = jnp.concatenate(heads_out, axis=1).astype(BF16)

    load_wo.wait()
    uw = D // sum(GROUPS)
    edges = [sum(GROUPS[:c]) for c in range(NC + 1)]

    def part_copy(c, i, owner, slot):
        units = pl.ds(edges[c], GROUPS[c])
        return pltpu.make_async_remote_copy(
            psend.at[units], precv.at[owner, units], xs.at[0], xr.at[slot, c],
            device_id={"heads": hp[i]}, device_id_type=MESH,
        )

    kv_wait(parts[0], kbuf.at[z, pl.ds(0, H - 1)], xs.at[0], z).wait_send()
    for c in range(NC):
        lo, hi = edges[c] * uw, edges[c + 1] * uw
        part = jnp.dot(merged, wo[:, lo:hi], preferred_element_type=F32)
        rounded = part.astype(BF16)
        for u in range(GROUPS[c]):
            psend[edges[c] + u] = rounded[:, u * uw : (u + 1) * uw]
        for i in range(len(hp)):
            part_copy(c, i, h, H - 2 - i).start()
        own[:, lo:hi] = x[:, lo:hi].astype(F32) + part
    kv_wait(parts[1], vbuf.at[z, pl.ds(0, H - 1)], xs.at[1], z).wait_send()
    for part in parts:
        kv_wait(part, part[0].at[pl.ds(0, N - 1)], part[1], z).wait_send()
    load_tp.wait()
    hr = rows // 2
    swaps = []
    square = jnp.zeros((rows, 1), F32)
    blocks = cols // 128
    lane = lax.broadcasted_iota(jnp.int32, (1, 128), 1)
    stays = [
        tp_ref[b : b + 1, :] == (strand * H + h) * cols + b * 128 + lane for b in range(blocks)
    ]

    def cross(values, b, forward):
        swapped = jnp.where(lane % 2 == 0, pltpu.roll(values, 127, 1), pltpu.roll(values, 1, 1))
        return jnp.where(stays[b] | forward, values, swapped)

    for c in range(NC):
        a, e = edges[c] * uw, edges[c + 1] * uw
        summed = own[:, a:e]
        for i, peer in enumerate(hp):
            part_copy(c, i, peer, i).wait_recv()
            summed = summed + jnp.concatenate(
                [precv[peer, u].astype(F32) for u in range(edges[c], edges[c + 1])], axis=1
            )
        hidden = summed.astype(BF16).astype(F32)
        square = square + jnp.sum(hidden * hidden, axis=1, keepdims=True)
        gained = (hidden * spread(gains[1], a // 128, (e - a) // 128)).astype(BF16)
        last = c == NC - 1
        for s in (other_strand, strand):
            part = jnp.dot(gained, wt[s, a:e, :], preferred_element_type=F32)
            if c > 0:
                part = lg[s] + part
            if not last:
                lg[s] = part
                continue
            logits = part * lax.rsqrt(square / D + 1e-06)
            for r in range(2):
                part = logits[r * hr : (r + 1) * hr]
                track = (jnp.maximum(part, 0.0) + jnp.log1p(jnp.exp(-jnp.abs(part)))).astype(BF16)
                if s is strand:
                    for b in range(blocks):
                        at = slice(b * 128, (b + 1) * 128)
                        out_ref[r * hr : (r + 1) * hr, at] = 0.5 * cross(
                            track[:, at].astype(F32), b, fwd
                        )
                    continue
                snd[r] = track
                cp = pltpu.make_async_remote_copy(
                    snd.at[r], rcv.at[r], ss, sr.at[r],
                    device_id={"strand": other_strand}, device_id_type=MESH,
                )
                cp.start()
                swaps.append(cp)
    sent = precv.at[pl.ds(0, H - 1)]
    pltpu.make_async_remote_copy(
        sent, sent, xs.at[0], xr.at[0, 0], device_id={"heads": hp[0]}, device_id_type=MESH
    ).wait_send()
    for r in range(2):
        swaps[r].wait_recv()
        for b in range(blocks):
            at = slice(b * 128, (b + 1) * 128)
            rr = slice(r * hr, (r + 1) * hr)
            out_ref[rr, at] = out_ref[rr, at] + 0.5 * cross(
                rcv[r, :, at].astype(F32), b, jnp.logical_not(fwd)
            )
    pltpu.make_async_remote_copy(
        snd, rcv, ss, sr.at[0], device_id={"strand": other_strand}, device_id_type=MESH
    ).wait_send()


def body(
    base_codes, embed_table, attn_gain, w_query, w_key, w_value, w_out, head_gain, w_tracks, track_pairs
):
    H = lax.axis_size("heads")
    N = lax.axis_size("pos")
    rows = base_codes.shape[0] // BIN
    dl = embed_table.shape[1]
    D = dl * H
    cols = w_tracks.shape[2]
    kvl = w_key.shape[1] + w_value.shape[1]
    NC, NX = len(GROUPS), 4 if dl >= 4 * 128 else 3
    vm = pl.BlockSpec(memory_space=pltpu.VMEM)
    hbm = pl.BlockSpec(memory_space=pl.ANY)
    dma = pltpu.SemaphoreType.DMA
    hm = max(H - 1, 1)
    tracks = pl.pallas_call(
        functools.partial(kernel, H, N, NC, NX),
        out_shape=pltpu.VMEM((rows, cols), F32),
        in_specs=[hbm] * 10,
        out_specs=vm,
        scratch_shapes=[
            pltpu.VMEM((cols // 128, 128), jnp.int32),
            pltpu.VMEM((rows, BIN), jnp.int32),
            pltpu.VMEM((2, D // 128, 128), F32),
            pltpu.VMEM(embed_table.shape, BF16),
            pltpu.VMEM(w_query.shape, BF16),
            pltpu.VMEM((kvl, D), BF16),
            pltpu.VMEM(w_out.shape, BF16),
            pltpu.VMEM(w_tracks.shape, BF16),
            pltpu.VMEM((2, D, cols), BF16),
            pltpu.VMEM((H, dl // 128, rows, 128), BF16),
            pltpu.VMEM((N, H, w_key.shape[1], rows), BF16),
            pltpu.VMEM((N, H, w_value.shape[1], rows), BF16),
            pltpu.VMEM((N, KDIM // 2, rows), F32),
            pltpu.VMEM((N, KDIM // 2, rows), F32),
            pltpu.VMEM((rows, D), F32),
            pltpu.VMEM((sum(GROUPS), rows, D // sum(GROUPS)), BF16),
            pltpu.VMEM((H, sum(GROUPS), rows, D // sum(GROUPS)), BF16),
            pltpu.VMEM((2, rows, cols), F32),
            pltpu.VMEM((2, rows // 2, cols), BF16),
            pltpu.VMEM((2, rows // 2, cols), BF16),
            dma((3 + NX,)),
            dma((2,)),
            dma((hm, NC)),
            dma,
            dma,
            dma((N,)),
            dma((N,)),
            dma,
            dma((2,)),
            pltpu.SemaphoreType.REGULAR,
            pltpu.SemaphoreType.REGULAR,
        ],
        compiler_params=pltpu.CompilerParams(
            collective_id=0, has_side_effects=True, vmem_limit_bytes=60 * 1024 * 1024
        ),
    )(
        base_codes.reshape(rows, BIN),
        embed_table,
        attn_gain.reshape(D // 128, 128),
        w_query,
        w_key.T,
        w_value.T,
        w_out,
        head_gain.reshape(D // 128, 128),
        w_tracks,
        track_pairs.reshape(cols // 128, 128),
    )
    return tracks


def solution(mesh):
    placed = (
        P(("groups", "pos")),
        P(None, "heads"),
        P(),
        P(None, "heads"),
        P(None, "heads"),
        P(None, "heads"),
        P("heads", None),
        P(),
        P(None, None, "heads"),
        P(("strand", "heads")),
    )
    return jax.shard_map(
        body,
        mesh=mesh,
        in_specs=placed,
        out_specs=P(("groups", "pos"), ("strand", "heads")),
        check_vma=False,
    )
```

```python
import functools
import math

import jax
import jax.numpy as jnp
from jax import lax
from jax.experimental import pallas as pl
from jax.experimental.pallas import tpu as pltpu
from jax.sharding import PartitionSpec as P

KDIM = 128
VDIM = 192
BIN = 128
F32 = jnp.float32
BF16 = jnp.bfloat16
MESH = pl.DeviceIdType.MESH
NT = (((1,), (1,)), ((), ()))
FIRST = 1
GROUPS = (1, 3, 4, 3, 1)


def spread(table, first, count):
    return jnp.concatenate([table[first + i : first + i + 1, :] for i in range(count)], axis=1)


def partner(z, step, N):
    if N & (N - 1):
        return lax.rem(z + step, N)
    bit = 1
    while bit < N:
        if step & bit:
            z = z + bit - 2 * bit * ((z // bit) % 2)
        bit *= 2
    return z


def kernel(
    H, N, NC, NX,
    codes_hbm, et_hbm, g1_hbm, wq_hbm, wk_hbm, wv_hbm, wo_hbm, g2_hbm, wt_hbm, tp_hbm,
    out_ref,
    tp_ref, codes_ref, gains, et, wq, wkv, wo, wraw, wt, xbuf, kbuf, vbuf, tabc, tabs, own, psend, precv, lg, snd, rcv,
    ls, xs, xr, ks, vs, kr, vr, ss, sr, ready, turn,
):
    h = lax.axis_index("heads")
    z = lax.axis_index("pos")
    strand = lax.axis_index("strand")
    rows = codes_hbm.shape[0]
    dl = et.shape[1]
    D = dl * H
    kl = wk_hbm.shape[0]
    kvl = wkv.shape[0]
    lh = wq.shape[1] // KDIM
    cols = wt.shape[2]
    total = rows * N

    hp = [lax.rem(h + i, H) for i in range(1, H)]
    zp = [partner(z, i, N) for i in range(1, N)]
    other_strand = 1 - strand

    def direct(p):
        return (4 * p < N) | (2 * (z - p) >= N) | ((strand == FIRST) & (z - p == 1))

    barrier = pltpu.get_barrier_semaphore()

    def greet(sem, up):
        for peer in zp:
            @pl.when(peer > z if up else peer < z)
            def _():
                for other in [h] + hp:
                    pl.semaphore_signal(
                        sem, inc=1, device_id={"pos": peer, "heads": other}, device_id_type=MESH
                    )

    greet(barrier, True)
    for peer in hp:
        pl.semaphore_signal(barrier, inc=1, device_id={"heads": peer}, device_id_type=MESH)
    pl.semaphore_signal(barrier, inc=1, device_id={"strand": other_strand}, device_id_type=MESH)

    xunits = dl // 128
    lead = max(1, xunits // 3)
    after = max(1, xunits // 6)
    xsizes = (lead, after, xunits - lead - after)
    xat = [sum(xsizes[:c]) for c in range(NX + 1)]
    load_codes = pltpu.make_async_copy(codes_hbm, codes_ref, ls.at[0])
    load_wq = pltpu.make_async_copy(wq_hbm, wq, ls.at[0])
    load_et = [
        pltpu.make_async_copy(
            et_hbm.at[:, pl.ds(xat[c] * 128, xsizes[c] * 128)],
            et.at[:, pl.ds(xat[c] * 128, xsizes[c] * 128)],
            ls.at[1 + c],
        )
        for c in range(NX)
    ]
    load_tp = pltpu.make_async_copy(tp_hbm, tp_ref, ls.at[1])
    load_wt = pltpu.make_async_copy(wt_hbm, wraw, ls.at[2])
    load_wo = pltpu.make_async_copy(wo_hbm, wo, ls.at[3])
    load_codes.start()
    for cp in load_et:
        cp.start()
    pltpu.make_async_copy(g1_hbm, gains.at[0], ls.at[1 + NX]).start()
    pltpu.make_async_copy(g2_hbm, gains.at[1], ls.at[1 + NX]).start()

    fwd = strand == 0
    width = 4 * BIN
    src_row = lax.broadcasted_iota(jnp.int32, (BIN, width), 0)
    place = lax.broadcasted_iota(jnp.int32, (BIN, width), 1) // 4
    want = jnp.where(fwd, place, BIN - 1 - place)
    expand = (src_row == want).astype(F32).astype(BF16)
    load_codes.wait()
    repeated = jnp.dot(codes_ref[...].astype(F32).astype(BF16), expand, preferred_element_type=F32)
    letter = lax.broadcasted_iota(jnp.int32, (rows, width), 1) % 4
    letter = jnp.where(fwd, letter, 3 - letter).astype(F32)
    onehot = (repeated == letter).astype(F32).astype(BF16)

    pltpu.make_async_copy(wk_hbm, wkv.at[pl.ds(0, kl), :], ls.at[2 + NX]).start()
    pltpu.make_async_copy(wv_hbm, wkv.at[pl.ds(kl, kvl - kl), :], ls.at[2 + NX]).start()
    load_wq.start()
    gate = max(NX - 2, 0)

    def x_copy(i, c):
        ref = xbuf.at[h, pl.ds(xat[c], xsizes[c])]
        return pltpu.make_async_remote_copy(
            ref, ref, xs.at[int(c > gate)], xr.at[H - 2 - i, int(c > gate)],
            device_id={"heads": hp[i]}, device_id_type=MESH,
        )

    def x_wait(part, i, count, first):
        units = pl.ds(0, xat[gate + 1]) if part == 0 else pl.ds(xat[gate + 1], xat[NX] - xat[gate + 1])
        ref = xbuf.at[pl.ds(first, count), units]
        return pltpu.make_async_remote_copy(
            ref, ref, xs.at[part], xr.at[i, part], device_id={"heads": hp[i]}, device_id_type=MESH
        )

    for c in range(NX):
        load_et[c].wait()
        part = jnp.dot(
            onehot, et[:, xat[c] * 128 : xat[c + 1] * 128], preferred_element_type=F32
        ).astype(BF16)
        for u in range(xsizes[c]):
            xbuf[h, xat[c] + u] = part[:, u * 128 : (u + 1) * 128]
        if c == 0:
            pl.semaphore_wait(barrier, len(hp) + 1 + z * H)
            greet(ready, False)

        @pl.when(strand == FIRST)
        def _():
            for i in range(len(hp)):
                x_copy(i, c).start()
    load_wt.start()
    load_wo.start()
    load_tp.start()

    half = KDIM // 2
    step = -math.log(10000.0) / half
    lane_pos = lax.broadcasted_iota(jnp.int32, (half, rows), 1)
    kinv = jnp.exp(lax.broadcasted_iota(jnp.int32, (half, rows), 0).astype(F32) * step)
    for p in range(N):
        pos = lane_pos + p * rows
        pos = jnp.where(fwd, pos, total - 1 - pos).astype(F32)
        tabc[p] = jnp.cos(pos * kinv)
        tabs[p] = jnp.sin(pos * kinv)
    qpos = lax.broadcasted_iota(jnp.int32, (rows, KDIM), 0) + z * rows
    qpos = jnp.where(fwd, qpos, total - 1 - qpos).astype(F32)
    qlane = lax.broadcasted_iota(jnp.int32, (rows, KDIM), 1)
    qang = qpos * jnp.exp((qlane % half).astype(F32) * step)
    qcos = jnp.cos(qang)
    qsin = jnp.where(qlane < half, -1.0, 1.0) * jnp.sin(qang)


    @pl.when(strand == FIRST)
    def _():
        x_wait(0, 0, H - 1, 0).wait_send()
        pl.semaphore_signal(turn, inc=1, device_id={"strand": other_strand}, device_id_type=MESH)

    @pl.when(strand != FIRST)
    def _():
        pl.semaphore_wait(turn, 1)
        for c in range(NX):
            for i in range(len(hp)):
                x_copy(i, c).start()


    pltpu.make_async_copy(gains, gains, ls.at[1 + NX]).wait()
    pltpu.make_async_copy(wkv, wkv, ls.at[2 + NX]).wait()
    load_wq.wait()
    kv_sum = jnp.zeros((kvl, rows), F32)
    q_sum = jnp.zeros((rows, lh * KDIM), F32)
    total_square = jnp.zeros((rows, 1), F32)
    for k, peer in enumerate([h] + hp):
        for c in range(NX):
            if k == 1 and c == 0:
                @pl.when(strand != FIRST)
                def _():
                    x_wait(0, 0, H - 1, 0).wait_send()

                x_wait(1, 0, H - 1, 0).wait_send()
            if k > 0 and c in (0, gate + 1):
                x_wait(int(c > gate), k - 1, 1, peer).wait_recv()
            piece = jnp.concatenate(
                [xbuf[peer, u].astype(F32) for u in range(xat[c], xat[c + 1])], axis=1
            )
            total_square = total_square + jnp.sum(piece * piece, axis=1, keepdims=True)
            first = peer * dl + xat[c] * 128
            gain = jnp.concatenate(
                [gains[0, pl.ds(first // 128 + j, 1), :] for j in range(xsizes[c])], axis=1
            )
            gained = (piece * gain).astype(BF16)
            at = pl.ds(pl.multiple_of(first, 128), xsizes[c] * 128)
            kv_sum = kv_sum + lax.dot_general(wkv[:, at], gained, NT, preferred_element_type=F32)
            if peer is hp[-1] and c == NX - 1:
                break
            q_sum = q_sum + jnp.dot(gained, wq[at, :], preferred_element_type=F32)
    scale = lax.rsqrt(total_square / D + 1e-06)
    scale_row = jnp.transpose(jnp.broadcast_to(scale, (rows, 128)))[:1, :]
    kv_own = (kv_sum * scale_row).astype(BF16)
    kbuf[z, h] = kv_own[:kl]
    vbuf[z, h] = kv_own[kl:]
    parts = ((kbuf, ks, kr, xs.at[0]), (vbuf, vs, vr, xs.at[1]))

    def kv_copy(part, p, hh, send, target):
        buf, _, recv, _ = part
        return pltpu.make_async_remote_copy(
            buf.at[p, hh], buf.at[p, hh], send, recv.at[p], device_id=target, device_id_type=MESH
        )

    def kv_wait(part, ref, send, p):
        return pltpu.make_async_remote_copy(
            ref, ref, send, part[2].at[p], device_id={"heads": hp[0]}, device_id_type=MESH
        )

    @pl.when(z < N - 1)
    def _():
        pl.semaphore_wait(ready, (N - 1 - z) * H)

    for i in range(N - 1):
        p = jnp.where(z <= i, i + 1, i)

        @pl.when(direct(p))
        def _():
            for part in parts:
                for other in hp:
                    kv_copy(part, z, h, part[1], {"pos": p, "heads": other}).start()

        for part in parts:
            kv_copy(part, z, h, part[1], {"pos": p}).start()
            if i == 0:
                for other in hp:
                    kv_copy(part, z, h, part[3], {"heads": other}).start()

    q_sum = q_sum + jnp.dot(gained, wq[at, :], preferred_element_type=F32)
    queries = (q_sum * scale).astype(BF16).astype(F32)
    rotated = []
    for a in range(lh):
        qa = queries[:, a * KDIM : (a + 1) * KDIM]
        rotated.append((qa * qcos + pltpu.roll(qa, half, 1) * qsin).astype(BF16))

    for part in parts:
        kv_wait(part, part[0].at[z, pl.ds(0, H - 1)], part[3], z).wait_recv()
        for i in range(N - 1):
            peer = jnp.where(z <= i, i + 1, i)

            @pl.when(jnp.logical_not(direct(peer)))
            def _():
                for other in hp:
                    kv_copy(part, z, other, part[1], {"pos": peer}).start()

    load_wt.wait()
    for i in range(0, D, 128):
        wt[:, i : i + 128, :] = jnp.swapaxes(wraw[i : i + 128], 0, 1)
    score_parts, vts = [[] for _ in range(lh)], []
    for p in [z] + zp:
        if p is not z:
            kv_wait(parts[0], kbuf.at[p], ks, p).wait_recv()
        kt = jnp.concatenate([kbuf[p, i] for i in range(H)], axis=0).astype(F32)
        lo, hi = kt[:half], kt[half:]
        kt = jnp.concatenate(
            [lo * tabc[p] - hi * tabs[p], hi * tabc[p] + lo * tabs[p]], axis=0
        ).astype(BF16)
        for a in range(lh):
            score_parts[a].append(
                jnp.dot(rotated[a], kt, preferred_element_type=F32) * KDIM ** (-0.5)
            )
    for p in [z] + zp:
        if p is not z:
            kv_wait(parts[1], vbuf.at[p], vs, p).wait_recv()
        vts.append(jnp.concatenate([vbuf[p, i] for i in range(H)], axis=0))
    vt = jnp.concatenate(vts, axis=1)
    x = jnp.concatenate([xbuf[i, u] for i in range(H) for u in range(xunits)], axis=1)
    heads_out = []
    for a in range(lh):
        scores = jnp.concatenate(score_parts[a], axis=1)
        top = jnp.max(scores, axis=1, keepdims=True)
        weights = jnp.exp(scores - top)
        weight_sum = jnp.sum(weights, axis=1, keepdims=True)
        mixed = lax.dot_general(weights.astype(BF16), vt, NT, preferred_element_type=F32)
        heads_out.append(mixed / weight_sum)
    merged = jnp.concatenate(heads_out, axis=1).astype(BF16)

    load_wo.wait()
    uw = D // sum(GROUPS)
    edges = [sum(GROUPS[:c]) for c in range(NC + 1)]

    def part_copy(c, i, owner, slot):
        units = pl.ds(edges[c], GROUPS[c])
        return pltpu.make_async_remote_copy(
            psend.at[units], precv.at[owner, units], xs.at[0], xr.at[slot, c],
            device_id={"heads": hp[i]}, device_id_type=MESH,
        )

    kv_wait(parts[0], kbuf.at[z, pl.ds(0, H - 1)], xs.at[0], z).wait_send()
    for c in range(NC):
        lo, hi = edges[c] * uw, edges[c + 1] * uw
        part = jnp.dot(merged, wo[:, lo:hi], preferred_element_type=F32)
        rounded = part.astype(BF16)
        for u in range(GROUPS[c]):
            psend[edges[c] + u] = rounded[:, u * uw : (u + 1) * uw]
        for i in range(len(hp)):
            part_copy(c, i, h, H - 2 - i).start()
        own[:, lo:hi] = x[:, lo:hi].astype(F32) + part
    kv_wait(parts[1], vbuf.at[z, pl.ds(0, H - 1)], xs.at[1], z).wait_send()
    for part in parts:
        kv_wait(part, part[0].at[pl.ds(0, N - 1)], part[1], z).wait_send()
    load_tp.wait()
    hr = rows // 2
    swaps = []
    square = jnp.zeros((rows, 1), F32)
    blocks = cols // 128
    lane = lax.broadcasted_iota(jnp.int32, (1, 128), 1)
    stays = [
        tp_ref[b : b + 1, :] == (strand * H + h) * cols + b * 128 + lane for b in range(blocks)
    ]

    def cross(values, b, forward):
        swapped = jnp.where(lane % 2 == 0, pltpu.roll(values, 127, 1), pltpu.roll(values, 1, 1))
        return jnp.where(stays[b] | forward, values, swapped)

    for c in range(NC):
        a, e = edges[c] * uw, edges[c + 1] * uw
        summed = own[:, a:e]
        for i, peer in enumerate(hp):
            part_copy(c, i, peer, i).wait_recv()
            summed = summed + jnp.concatenate(
                [precv[peer, u].astype(F32) for u in range(edges[c], edges[c + 1])], axis=1
            )
        hidden = summed.astype(BF16).astype(F32)
        square = square + jnp.sum(hidden * hidden, axis=1, keepdims=True)
        gained = (hidden * spread(gains[1], a // 128, (e - a) // 128)).astype(BF16)
        last = c == NC - 1
        for s in (other_strand, strand):
            part = jnp.dot(gained, wt[s, a:e, :], preferred_element_type=F32)
            if c > 0:
                part = lg[s] + part
            if not last:
                lg[s] = part
                continue
            logits = part * lax.rsqrt(square / D + 1e-06)
            for r in range(2):
                part = logits[r * hr : (r + 1) * hr]
                track = (jnp.maximum(part, 0.0) + jnp.log1p(jnp.exp(-jnp.abs(part)))).astype(BF16)
                if s is strand:
                    for b in range(blocks):
                        at = slice(b * 128, (b + 1) * 128)
                        out_ref[r * hr : (r + 1) * hr, at] = 0.5 * cross(
                            track[:, at].astype(F32), b, fwd
                        )
                    continue
                snd[r] = track
                cp = pltpu.make_async_remote_copy(
                    snd.at[r], rcv.at[r], ss, sr.at[r],
                    device_id={"strand": other_strand}, device_id_type=MESH,
                )
                cp.start()
                swaps.append(cp)
    sent = precv.at[pl.ds(0, H - 1)]
    pltpu.make_async_remote_copy(
        sent, sent, xs.at[0], xr.at[0, 0], device_id={"heads": hp[0]}, device_id_type=MESH
    ).wait_send()
    for r in range(2):
        swaps[r].wait_recv()
        for b in range(blocks):
            at = slice(b * 128, (b + 1) * 128)
            rr = slice(r * hr, (r + 1) * hr)
            out_ref[rr, at] = out_ref[rr, at] + 0.5 * cross(
                rcv[r, :, at].astype(F32), b, jnp.logical_not(fwd)
            )
    pltpu.make_async_remote_copy(
        snd, rcv, ss, sr.at[0], device_id={"strand": other_strand}, device_id_type=MESH
    ).wait_send()


def body(
    base_codes, embed_table, attn_gain, w_query, w_key, w_value, w_out, head_gain, w_tracks, track_pairs
):
    H = lax.axis_size("heads")
    N = lax.axis_size("pos")
    rows = base_codes.shape[0] // BIN
    dl = embed_table.shape[1]
    D = dl * H
    cols = w_tracks.shape[2]
    kvl = w_key.shape[1] + w_value.shape[1]
    NC, NX = len(GROUPS), 3
    vm = pl.BlockSpec(memory_space=pltpu.VMEM)
    hbm = pl.BlockSpec(memory_space=pl.ANY)
    dma = pltpu.SemaphoreType.DMA
    hm = max(H - 1, 1)
    tracks = pl.pallas_call(
        functools.partial(kernel, H, N, NC, NX),
        out_shape=pltpu.VMEM((rows, cols), F32),
        in_specs=[hbm] * 10,
        out_specs=vm,
        scratch_shapes=[
            pltpu.VMEM((cols // 128, 128), jnp.int32),
            pltpu.VMEM((rows, BIN), jnp.int32),
            pltpu.VMEM((2, D // 128, 128), F32),
            pltpu.VMEM(embed_table.shape, BF16),
            pltpu.VMEM(w_query.shape, BF16),
            pltpu.VMEM((kvl, D), BF16),
            pltpu.VMEM(w_out.shape, BF16),
            pltpu.VMEM(w_tracks.shape, BF16),
            pltpu.VMEM((2, D, cols), BF16),
            pltpu.VMEM((H, dl // 128, rows, 128), BF16),
            pltpu.VMEM((N, H, w_key.shape[1], rows), BF16),
            pltpu.VMEM((N, H, w_value.shape[1], rows), BF16),
            pltpu.VMEM((N, KDIM // 2, rows), F32),
            pltpu.VMEM((N, KDIM // 2, rows), F32),
            pltpu.VMEM((rows, D), F32),
            pltpu.VMEM((sum(GROUPS), rows, D // sum(GROUPS)), BF16),
            pltpu.VMEM((H, sum(GROUPS), rows, D // sum(GROUPS)), BF16),
            pltpu.VMEM((2, rows, cols), F32),
            pltpu.VMEM((2, rows // 2, cols), BF16),
            pltpu.VMEM((2, rows // 2, cols), BF16),
            dma((3 + NX,)),
            dma((2,)),
            dma((hm, NC)),
            dma,
            dma,
            dma((N,)),
            dma((N,)),
            dma,
            dma((2,)),
            pltpu.SemaphoreType.REGULAR,
            pltpu.SemaphoreType.REGULAR,
        ],
        compiler_params=pltpu.CompilerParams(
            collective_id=0, has_side_effects=True, vmem_limit_bytes=60 * 1024 * 1024
        ),
    )(
        base_codes.reshape(rows, BIN),
        embed_table,
        attn_gain.reshape(D // 128, 128),
        w_query,
        w_key.T,
        w_value.T,
        w_out,
        head_gain.reshape(D // 128, 128),
        w_tracks,
        track_pairs.reshape(cols // 128, 128),
    )
    return tracks


def solution(mesh):
    placed = (
        P(("groups", "pos")),
        P(None, "heads"),
        P(),
        P(None, "heads"),
        P(None, "heads"),
        P(None, "heads"),
        P("heads", None),
        P(),
        P(None, None, "heads"),
        P(("strand", "heads")),
    )
    return jax.shard_map(
        body,
        mesh=mesh,
        in_specs=placed,
        out_specs=P(("groups", "pos"), ("strand", "heads")),
        check_vma=False,
    )
```
